32 devices in a mesh: member: 4 (over x, core), space: 8 (over z, y).
Axes of the slice: x: 2, y: 2, z: 4, core: 2. Of those that a mesh axis runs over, the one named last changes fastest.
Arguments:
- members: float32 [16, 16, 2, 368, 384], P('member', None, None, 'space'), may hold values from -6 to 6
- target: float32 [16, 2, 368, 384], P('member', None, 'space'), may hold values from -6 to 6
- order_table: int32 [368], replicated, may hold values from 0 to 367, each once
Outputs:
- field_grad: float32 [16, 16, 368, 720], P('member', None, 'space')
The draws below stay inside these ranges and needn't reach their ends.
Inputs may be any that keep to these rules, and one draw needn't show every extreme that they name: Slot p of the order dimension of members and target holds order order_table[p]; each of 0 to 367 appears once, and orders above 360 are empty slots.
All inputs are finite; a program needn't handle non-finite values.
Results may differ from the reference program's by a relative error of at most 0.0003.
Values sent between devices are 32-bit elements; how exact they have to be, the bound alone decides.
No kernel may reach another device: no remote copies, remote signals or barrier semaphores. Data moves between devices by JAX's collectives and lax.ppermute only.
A program may use at most 192 MiB of HBM per device.

```python
import math
import jax
import jax.numpy as jnp
from jax import lax

MEMBERS = 16
CHANNELS = 16
LMAX = 360
NLAT = 361
NLON = 720
M_PAD = 368
L_PAD = 384
NLAT_PAD = 368


def level_of(own_key, extent, split, least, top_value):
    def one(axis_at, blocks):
        draws = jax.random.uniform(jax.random.fold_in(jax.random.fold_in(own_key, 6), axis_at), (blocks,), jnp.float32, least / len(split), top_value / len(split))
        return jnp.repeat(jnp.exp(draws), extent[axis_at] // blocks).reshape((-1,) + (1,) * (len(extent) - axis_at - 1))

    gain = one(*split[0])
    for cut in split[1:]:
        gain = gain * one(*cut)
    return gain


def centred(stream_key, extent, scale, bound, shards=(), kind=jnp.bfloat16):
    level = level_of(stream_key, extent, shards, -0.22, 0.18) if shards else 1.0
    drawn = jax.random.normal(stream_key, extent, jnp.float32) * scale * level
    return jnp.minimum(jnp.maximum(drawn, -bound), bound).astype(kind)


def setup_inputs(seed: int = 0) -> dict:
    arg_keys = jax.random.split(jax.random.key(seed), 4)
    members = centred(arg_keys[0], (MEMBERS, CHANNELS, 2, M_PAD, L_PAD), 1.0, 6.0, ((0, 4), (3, 8)), jnp.float32)
    target = centred(arg_keys[1], (CHANNELS, 2, M_PAD, L_PAD), 1.0, 6.0, ((0, 4), (2, 8)), jnp.float32)
    order_table = jax.random.permutation(arg_keys[2], M_PAD).astype(jnp.int32)
    return {"members": members, "target": target, "order_table": order_table}


smooth_eps = 0.01
log_gamma_half = 0.5 * math.log(math.pi) - math.log(2.0)

def legendre_table(orders, lmax, nlat, lpad, nlatp):
    rows = jnp.arange(nlatp, dtype=jnp.int32)
    row_f = rows.astype(jnp.float32)
    span = float(nlat - 1)
    theta = jnp.pi * row_f / span
    nearest = jnp.clip(jnp.minimum(row_f, span - row_f), 0.0, None)
    sines = jnp.sin(jnp.pi * nearest / span)
    cosines = jnp.cos(theta)
    lat_weight = jnp.where(rows < nlat, sines, 0.0)
    order_i = jnp.minimum(orders, lmax).astype(jnp.int32)
    order_f = order_i.astype(jnp.float32)
    log_base = 0.5 * (math.log(1.0 / (4.0 * math.pi)) + lax.lgamma(order_f + 1.5) - log_gamma_half - lax.lgamma(order_f + 1.0))
    order_col = order_i[:, None]
    order_fc = order_f[:, None]
    log_sine = jnp.log(jnp.where(sines > 0.0, sines, 1.0))
    polar_zero = (sines[None, :] <= 0.0) & (order_fc > 0.0)
    start_value = jnp.where(polar_zero, 0.0, 1.0)
    start_scale = jnp.where(polar_zero, 0.0, log_base[:, None] + order_fc * log_sine[None, :])

    def step(carry, degree):
        prev, prev2, scale = carry
        deg_f = degree.astype(jnp.float32)
        coef_a = jnp.sqrt(jnp.maximum(4.0 * deg_f * deg_f - 1.0, 1.0) / jnp.maximum(deg_f * deg_f - order_fc * order_fc, 1.0))
        lower = deg_f - 1.0
        coef_b = jnp.sqrt(jnp.maximum(lower * lower - order_fc * order_fc, 0.0) / jnp.maximum(4.0 * lower * lower - 1.0, 1.0))
        recur = coef_a * (cosines[None, :] * prev - coef_b * prev2)
        at_start = degree == order_col
        current = jnp.where(degree < order_col, 0.0, jnp.where(at_start, start_value, recur))
        scale_now = jnp.where(at_start, start_scale, scale)
        shifted = jnp.where(at_start, 0.0, prev)
        largest = jnp.maximum(jnp.abs(current), jnp.abs(shifted))
        divisor = jnp.where(largest > 0.0, largest, 1.0)
        current_n = current / divisor
        shifted_n = shifted / divisor
        scale_n = scale_now + jnp.log(divisor)
        return ((current_n, shifted_n, scale_n), current_n * jnp.exp(scale_n))
    zeros = jnp.zeros((orders.shape[0], nlatp), jnp.float32)
    _, stacked = lax.scan(step, (zeros, zeros, zeros), jnp.arange(lpad, dtype=jnp.int32), unroll=16)
    table = jnp.transpose(stacked, (1, 0, 2))
    degrees = jnp.arange(lpad, dtype=jnp.int32)
    valid = (degrees[None, :] <= lmax) & (orders[:, None] <= lmax)
    return jnp.where(valid[:, :, None], table, 0.0) * lat_weight[None, None, :]

def loss_weight(orders, lmax, lpad):
    degrees = jnp.arange(lpad, dtype=jnp.int32)[None, :]
    order_col = orders[:, None]
    valid = (degrees >= order_col) & (degrees <= lmax) & (order_col <= lmax)
    doubled = jnp.where(order_col == 0, 1.0, 2.0)
    return jnp.where(valid, doubled, 0.0).astype(jnp.float32)

def pair_gradient(rows, ensemble, targets, orders, lmax):
    count = ensemble.shape[0]
    weight = loss_weight(orders, lmax, ensemble.shape[4])
    diff = rows - targets[None]
    size = jnp.sqrt(lax.optimization_barrier(jnp.sum(diff * diff, axis=2, keepdims=True)) + smooth_eps)

    def against(single):
        delta = single[None] - ensemble
        dist = jnp.sqrt(lax.optimization_barrier(jnp.sum(delta * delta, axis=2, keepdims=True)) + smooth_eps)
        return lax.optimization_barrier(jnp.sum(delta / dist, axis=0))
    spread = lax.map(against, rows)
    return (diff / size / count - spread / (count * (count - 1))) * weight

def to_latitudes(grads, table):
    return jnp.einsum('ecrml,mlj->ecjrm', grads, table, precision=lax.Precision.HIGHEST)

def longitude_basis(orders, nlon, lmax):
    cols = jnp.arange(nlon, dtype=jnp.int32)
    phase = orders[:, None] * cols[None, :] % nlon
    angle = 2.0 * jnp.pi * phase.astype(jnp.float32) / nlon
    valid = (orders <= lmax)[:, None]
    scale = 2.0 * jnp.pi / nlon
    cosine = jnp.where(valid, jnp.cos(angle), 0.0) * scale
    sine = jnp.where(valid, -jnp.sin(angle), 0.0) * scale
    return jnp.stack([cosine, sine], axis=0)

def to_longitudes(lat_grad, basis):
    ens, chans, lats, parts, slots = lat_grad.shape
    flat = lat_grad.reshape(ens * chans * lats, parts * slots)
    result = jnp.dot(flat, basis.reshape(parts * slots, basis.shape[2]), precision=lax.Precision.HIGHEST, preferred_element_type=jnp.float32)
    return result.reshape(ens, chans, lats, basis.shape[2])

def reference(members, target, order_table):
    table = legendre_table(order_table, LMAX, NLAT, L_PAD, NLAT_PAD)
    basis = longitude_basis(order_table, NLON, LMAX)

    def per_channel(channel):
        ensemble = lax.dynamic_slice_in_dim(members, channel, 1, 1)
        targets = lax.dynamic_slice_in_dim(target, channel, 1, 0)
        grads = pair_gradient(ensemble, ensemble, targets, order_table, LMAX)
        return to_longitudes(to_latitudes(grads, table), basis)[:, 0]
    result = lax.map(per_channel, jnp.arange(CHANNELS, dtype=jnp.int32))
    return jnp.transpose(result, (1, 0, 2, 3))
```

```python
import functools
import math

import jax
import jax.numpy as jnp
from jax import lax
from jax.experimental import pallas as pl
from jax.experimental.pallas import tpu as pltpu
from jax.sharding import PartitionSpec as P


LMAX = 360
NLAT = 361
NLON = 720

EPS = 0.01
LOG_GAMMA_HALF = 0.5 * math.log(math.pi) - math.log(2.0)
STEP_EXP = 64.0
SMALL = 2.0**-64
BIG = 2.0**32
PAD = 8
VMEM_LIMIT = 60 * 1024 * 1024


def round_up(value, multiple):
    return (value + multiple - 1) // multiple * multiple


def split(value):
    high = value.astype(jnp.bfloat16)
    low = (value - high.astype(jnp.float32)).astype(jnp.bfloat16)
    return high, low


def dot(a, b, dims=(((1,), (0,)), ((), ()))):
    return lax.dot_general(a, b, dims, preferred_element_type=jnp.float32)


def table_kernel(step_ref, inv_ref, order_ref, value_ref, scale_ref, cos_ref, high_ref, low_ref, rows_ref):
    group, width = value_ref.shape
    degrees = high_ref.shape[1]
    pitch = degrees + PAD
    order = order_ref[...]
    order_sq = order * order
    cosine = jnp.broadcast_to(cos_ref[0:1, :], (group, width))

    def wide(column):
        return jnp.concatenate([column] * (width // 128), axis=1)

    order_w = wide(order)

    def factors(scale):
        one = jnp.where(scale < -0.5, jnp.where(scale < -2.5, 0.0, SMALL), 1.0)
        two = jnp.where(scale < -1.5, SMALL, 1.0)
        return one, two

    def block(index, carry):
        prev, prev2, scale, root, gap = carry
        big = (jnp.maximum(jnp.abs(prev), jnp.abs(prev2)) > BIG) & (scale < -0.5)
        prev = jnp.where(big, prev * SMALL, prev)
        prev2 = jnp.where(big, prev2 * SMALL, prev2)
        scale = jnp.where(big, scale + 1.0, scale)
        one, two = factors(scale)
        for sub in range(8):
            degree = index * 8 + sub
            deg_f = degree.astype(jnp.float32)
            gap_now = deg_f * deg_f - order_sq
            safe = jnp.maximum(gap_now, 1.0)
            root_now = lax.rsqrt(safe)
            root_now = root_now * (1.5 - 0.5 * safe * root_now * root_now)
            coef_a = step_ref[degree] * root_now
            coef_b = jnp.maximum(gap, 0.0) * root * inv_ref[degree]
            current = wide(coef_a) * (cosine * prev - wide(coef_b) * prev2)
            current = jnp.where(order_w == deg_f, value_ref[...], current)
            shown = (current * one) * two
            for first in range(0, group, 8):
                for lane in range(0, width, 128):
                    rows_ref[lane // 128, pl.ds(first * pitch + degree, 8, pitch), :] = shown[
                        first : first + 8, lane : lane + 128
                    ]
            prev2 = prev
            prev = current
            root, gap = root_now, gap_now
        return prev, prev2, scale, root, gap

    zeros = jnp.zeros((group, width), jnp.float32)
    lax.fori_loop(
        0,
        degrees // 8,
        block,
        (zeros, zeros, scale_ref[...], jnp.ones_like(order), jnp.zeros_like(order)),
    )

    def convert(index, _):
        keep = lax.broadcasted_iota(jnp.int32, (degrees, 128), 0) <= LMAX
        start = pl.multiple_of(index * pitch, 8)
        for tile in range(width // 128):
            value = jnp.where(keep, rows_ref[tile, pl.ds(start, degrees), :], 0.0)
            high, low = split(value)
            lanes = slice(tile * 128, tile * 128 + 128)
            high_ref[index, :, lanes] = high
            low_ref[index, :, lanes] = low
        return 0

    lax.fori_loop(0, group, convert, 0)


def legendre_tables(orders, degrees, lats, valid):
    count = orders.shape[0]
    width = lats.shape[0]
    span = float(NLAT - 1)
    lat_f = lats.astype(jnp.float32)
    nearest = jnp.clip(jnp.minimum(lat_f, span - lat_f), 0.0, None)
    inside = valid & (nearest > 0.0)
    sines = jnp.where(inside, jnp.sin(jnp.pi * nearest / span), 1.0)
    cosines = jnp.cos(jnp.pi * lat_f / span)
    order_f = jnp.minimum(orders, LMAX).astype(jnp.float32)
    log_base = 0.5 * (
        math.log(1.0 / (4.0 * math.pi))
        + lax.lgamma(order_f + 1.5)
        - LOG_GAMMA_HALF
        - lax.lgamma(order_f + 1.0)
    )
    start = (log_base[:, None] + order_f[:, None] * jnp.log(sines)[None, :]) / math.log(2.0)
    scale = jnp.minimum(jnp.floor(start / STEP_EXP + 0.5), 0.0)
    weight = jnp.where(orders > LMAX, 0.0, jnp.where(orders == 0, 1.0, 2.0)).astype(jnp.float32)
    value = jnp.exp2(start - STEP_EXP * scale) * jnp.where(inside, sines, 0.0)[None, :]
    value = value * weight[:, None]
    square = jnp.arange(degrees, dtype=jnp.float32) ** 2
    step = jnp.sqrt(jnp.maximum(4.0 * square - 1.0, 1.0))
    inverse = 1.0 / jnp.concatenate([jnp.ones((1,), jnp.float32), step[:-1]])
    group = 8
    order_cols = jnp.broadcast_to(order_f[:, None], (count, 128))
    cos_rows = jnp.broadcast_to(cosines[None, :], (8, width))
    rows = lambda cols: pl.BlockSpec((group, cols), lambda g, *_: (g, 0))
    out = pl.BlockSpec((group, degrees, width), lambda g, *_: (g, 0, 0))
    shape = jax.ShapeDtypeStruct((count, degrees, width), jnp.bfloat16)
    return pl.pallas_call(
        table_kernel,
        name="legendre_table",
        out_shape=(shape, shape),
        grid_spec=pltpu.PrefetchScalarGridSpec(
            num_scalar_prefetch=2,
            grid=(count // group,),
            in_specs=[rows(128), rows(width), rows(width), pl.BlockSpec((8, width), lambda g, *_: (0, 0))],
            out_specs=(out, out),
            scratch_shapes=[pltpu.VMEM((width // 128, group * (degrees + PAD), 128), jnp.float32)],
        ),
        compiler_params=pltpu.CompilerParams(vmem_limit_bytes=VMEM_LIMIT),
        cost_estimate=pl.CostEstimate(
            flops=10 * count * degrees * width,
            transcendentals=count * degrees,
            bytes_accessed=4 * count * degrees * width,
        ),
    )(step, inverse, order_cols, value, scale, cos_rows)


def gradient_kernel(slots, me_ref, *refs):
    blocks = refs[:-8]
    target_ref, high_ref, low_ref, band_ref, out_ref, sums_ref, grads_ref, lat_ref = refs[-8:]
    groups = len(blocks)
    local = blocks[0].shape[0]
    degrees = target_ref.shape[2]
    width = high_ref.shape[2]
    spaces = out_ref.shape[1]
    width_out = out_ref.shape[3]
    count = groups * local
    rows = 2 * count
    pitch = rows + PAD
    per = 2 * local
    lanes_of = width // spaces
    first_slot = pl.program_id(0) * 8
    live = lax.broadcasted_iota(jnp.int32, (8, 128), 0) + first_slot < slots
    share = 1.0 / count
    pair_share = 1.0 / (count * (count - 1))

    def lane_tile(tile, _):
        lanes = pl.ds(pl.multiple_of(tile * 128, 128), 128)

        def coef(index):
            ref = blocks[index // local]
            return ref[index % local, 0, :, lanes], ref[index % local, 1, :, lanes]

        for group in range(groups):
            base = group * local
            mine = [coef(base + e) for e in range(local)]
            if group == 0:
                total = [[jnp.zeros((8, 128), jnp.float32) for _ in range(2)] for _ in range(local)]
            else:
                total = [[sums_ref[2 * (base + e) + r] for r in range(2)] for e in range(local)]

            def force(a, b):
                real, imag = a[0] - b[0], a[1] - b[1]
                inverse = lax.rsqrt(real * real + (imag * imag + EPS))
                return real * inverse, imag * inverse

            for e in range(local):
                for f in range(e + 1, local):
                    pull = force(mine[e], mine[f])
                    for r in range(2):
                        total[e][r] = total[e][r] + pull[r]
                        total[f][r] = total[f][r] - pull[r]
            for other in range(base + local, count):
                theirs = coef(other)
                sums = None if group == 0 else [sums_ref[2 * other + r] for r in range(2)]
                for e in range(local):
                    pull = force(mine[e], theirs)
                    for r in range(2):
                        total[e][r] = total[e][r] + pull[r]
                    if sums is None:
                        sums = [-pull[0], -pull[1]]
                    else:
                        sums = [sums[0] - pull[0], sums[1] - pull[1]]
                for r in range(2):
                    sums_ref[2 * other + r] = sums[r]
            goal = (target_ref[0, :, lanes], target_ref[1, :, lanes])
            owner = lax.rem(me_ref[0] + (groups - group), groups)
            for e in range(local):
                pull = force(mine[e], goal)
                for r in range(2):
                    grad = pull[r] * share - total[e][r] * pair_share
                    grad = jnp.where(live, grad, 0.0)
                    grads_ref[tile, pl.ds(owner * per + r * local + e, 8, pitch), :] = grad
        return 0

    lax.fori_loop(0, degrees // 128, lane_tile, 0)

    def transform(slot, _):
        start = pl.multiple_of(slot * pitch, 8)
        grad = jnp.concatenate(
            [grads_ref[tile, pl.ds(start, rows), :] for tile in range(degrees // 128)], axis=1
        )
        high, low = split(grad)
        both = dot(jnp.concatenate([high, low], axis=0), high_ref[slot])
        lat = both[:rows] + both[rows:] + dot(high, low_ref[slot])
        for tile in range(width // 128):
            lat_ref[tile, pl.ds(start, rows), :] = lat[:, tile * 128 : tile * 128 + 128]
        return 0

    lax.fori_loop(0, 8, transform, 0, unroll=2)

    band = band_ref[...]

    def load(group, row):
        parts = [
            lat_ref[tile, pl.ds(group * per + row, 8, pitch), :] for tile in range(width // 128)
        ]
        return jnp.concatenate(parts, axis=1)

    def scatter(group, _):
        source = [load(group, row) for row in range(per)]
        if spaces == per and width == width_out:
            distance = per // 2
            while distance:
                upper = (band & distance) != 0
                for i in range(per):
                    if i & distance:
                        continue
                    j = i | distance
                    shift = distance * lanes_of
                    from_j = pltpu.roll(source[j], shift, 1)
                    from_i = pltpu.roll(source[i], width - shift, 1)
                    source[i], source[j] = (
                        jnp.where(upper, from_j, source[i]),
                        jnp.where(upper, source[j], from_i),
                    )
                distance //= 2
            for space in range(spaces):
                out_ref[group, space] = source[space]
        else:
            for space in range(spaces):
                value = jnp.zeros((8, width_out), jnp.float32)
                for row in range(per):
                    shift = (row - space) * lanes_of % width
                    moved = source[row] if shift == 0 else pltpu.roll(source[row], shift, 1)
                    value = jnp.where(band[:, :width_out] == row, moved[:, :width_out], value)
                out_ref[group, space] = value
        return 0

    lax.fori_loop(0, groups, scatter, 0)


def lat_payload(me, parts, targets, channel, high, low, spaces):
    local, _, slots, degrees = parts[0].shape
    groups = len(parts)
    padded, _, width = high.shape
    per = 2 * local
    lanes_of = width // spaces
    width_out = round_up(per * lanes_of, 128)
    count = groups * local
    band = jnp.broadcast_to((jnp.arange(width, dtype=jnp.int32) // lanes_of)[None], (8, width))
    part_spec = pl.BlockSpec((local, 2, 8, degrees), lambda g, *_: (0, 0, g, 0))
    table_spec = pl.BlockSpec((8, degrees, width), lambda g, *_: (g, 0, 0))
    pairs = count * (count + 1) // 2
    return pl.pallas_call(
        functools.partial(gradient_kernel, slots),
        name="loss_gradient",
        out_shape=jax.ShapeDtypeStruct((groups, spaces, padded, width_out), jnp.float32),
        grid_spec=pltpu.PrefetchScalarGridSpec(
            num_scalar_prefetch=1,
            grid=(padded // 8,),
            in_specs=[part_spec] * groups
            + [
                pl.BlockSpec((None, 2, 8, degrees), lambda g, *_: (channel, 0, g, 0)),
                table_spec,
                table_spec,
                pl.BlockSpec((8, width), lambda g, *_: (0, 0)),
            ],
            out_specs=pl.BlockSpec((groups, spaces, 8, width_out), lambda g, *_: (0, 0, g, 0)),
            scratch_shapes=[
                pltpu.VMEM((2 * count, 8, 128), jnp.float32),
                pltpu.VMEM((degrees // 128, 8 * (2 * count + PAD), 128), jnp.float32),
                pltpu.VMEM((width // 128, 8 * (2 * count + PAD), 128), jnp.float32),
            ],
        ),
        compiler_params=pltpu.CompilerParams(vmem_limit_bytes=VMEM_LIMIT),
        cost_estimate=pl.CostEstimate(
            flops=6 * 2 * count * padded * degrees * width,
            transcendentals=pairs * padded * degrees,
            bytes_accessed=4 * padded * degrees * width + 16 * count * padded * degrees,
        ),
    )(me, *parts, targets, high, low, band)


def longitude_kernel(got_ref, high_ref, low_ref, out_ref):
    half = out_ref.shape[0]
    value = got_ref[...].T
    both = jnp.concatenate([value[:half], value[half : 2 * half]], axis=1)
    high, low = split(both)
    out_ref[...] = (
        dot(high, high_ref[...]) + dot(low, high_ref[...]) + dot(high, low_ref[...])
    )


def to_longitudes(received, high, low, half):
    groups, depth, width = received.shape
    whole = lambda shape: pl.BlockSpec(shape, lambda g: (0, 0))
    return pl.pallas_call(
        longitude_kernel,
        name="longitudes",
        out_shape=jax.ShapeDtypeStruct((groups, half, NLON), jnp.float32),
        grid=(groups,),
        in_specs=[
            pl.BlockSpec((None, depth, width), lambda g: (g, 0, 0)),
            whole(high.shape),
            whole(low.shape),
        ],
        out_specs=pl.BlockSpec((None, half, NLON), lambda g: (g, 0, 0)),
        compiler_params=pltpu.CompilerParams(vmem_limit_bytes=VMEM_LIMIT),
        cost_estimate=pl.CostEstimate(
            flops=6 * groups * half * 2 * depth * NLON,
            transcendentals=0,
            bytes_accessed=4 * groups * (depth * width + half * NLON),
        ),
    )(received, high, low)


def merge_kernel(lats, *refs):
    ins, out_ref, wide_ref = refs[:-2], refs[-2], refs[-1]
    chunks = len(ins)
    groups = ins[0].shape[0]
    channels = groups * chunks
    padded = ins[0].shape[1]
    pitch = channels + PAD
    for group in range(groups):
        for chunk in range(chunks):
            channel = group * chunks + chunk
            for first in range(0, padded, 8):
                for lane in range(0, NLON, 128):
                    size = min(128, NLON - lane)
                    value = ins[chunk][group, first : first + 8, lane : lane + size]
                    if size < 128:
                        value = jnp.concatenate([value, jnp.zeros((8, 128 - size), jnp.float32)], axis=1)
                    wide_ref[lane // 128, pl.ds(first * pitch + channel, 8, pitch), :] = value
    for lane in range(0, NLON, 128):
        size = min(128, NLON - lane)
        for lat in range(lats):
            out_ref[lat * channels : (lat + 1) * channels, lane : lane + size] = wide_ref[
                lane // 128, lat * pitch : lat * pitch + channels, :size
            ]


def merge(parts, local, lats, lanes_of):
    groups = parts[0].shape[0]
    channels = groups * len(parts)
    padded = round_up(lanes_of, 8)
    parts = [
        part if padded == lanes_of else jnp.pad(
            part.reshape(groups, local, lanes_of, NLON), ((0, 0), (0, 0), (0, padded - lanes_of), (0, 0))
        ).reshape(groups, local * padded, NLON)
        for part in parts
    ]
    out = pl.pallas_call(
        functools.partial(merge_kernel, lats),
        name="merge_channels",
        out_shape=jax.ShapeDtypeStruct((local, lats * channels, NLON), jnp.float32),
        grid=(local,),
        in_specs=[pl.BlockSpec((groups, padded, NLON), lambda e: (0, e, 0))] * len(parts),
        out_specs=pl.BlockSpec((None, lats * channels, NLON), lambda e: (e, 0, 0)),
        scratch_shapes=[pltpu.VMEM((pl.cdiv(NLON, 128), padded * (channels + PAD), 128), jnp.float32)],
        compiler_params=pltpu.CompilerParams(vmem_limit_bytes=VMEM_LIMIT),
        cost_estimate=pl.CostEstimate(
            flops=0, transcendentals=0, bytes_accessed=8 * local * lats * channels * NLON
        ),
    )(*parts)
    return out.reshape(local, lats, channels, NLON).transpose(0, 2, 1, 3)


def longitude_basis(orders):
    cols = jnp.arange(NLON, dtype=jnp.int32)
    phase = orders[:, None] * cols[None, :] % NLON
    angle = 2.0 * jnp.pi * phase.astype(jnp.float32) / NLON
    valid = (orders <= LMAX)[:, None]
    scale = 2.0 * jnp.pi / NLON
    cosine = jnp.where(valid, jnp.cos(angle), 0.0) * scale
    sine = jnp.where(valid, -jnp.sin(angle), 0.0) * scale
    value = jnp.concatenate([cosine, sine], axis=0)
    high = lax.reduce_precision(value, 8, 7)
    return high.astype(jnp.bfloat16), (value - high).astype(jnp.bfloat16)


def shards(members, target, order_table):
    local, channels, _, slots, degrees = members.shape
    spaces = lax.axis_size("space")
    groups = lax.axis_size("member")
    chunks = channels // groups
    me = lax.axis_index("member")
    padded = round_up(slots, 16)
    lats = (NLAT + spaces - 1) // spaces
    width = round_up(spaces * lats, 128)
    lanes_of = width // spaces

    by_device = jnp.pad(
        order_table.reshape(spaces, slots), ((0, 0), (0, padded - slots)), constant_values=LMAX + 1
    )
    mine = lax.dynamic_index_in_dim(by_device, lax.axis_index("space"), 0, keepdims=False)
    column = jnp.arange(width, dtype=jnp.int32)
    inner = column % lanes_of
    lat_index = column // lanes_of * lats + inner
    valid = (inner < lats) & (lat_index < NLAT)

    def pieces(source, chunk):
        result = []
        for step in range(groups):
            channel = lax.rem(me + step, groups) * chunks + chunk
            result.append(lax.dynamic_index_in_dim(source, channel, 1, keepdims=False))
        return result

    def exchange(cut):
        return [cut[0]] + [
            lax.ppermute(cut[step], "member", [(i, (i + step) % groups) for i in range(groups)])
            for step in range(1, groups)
        ]

    high, low = legendre_tables(mine, degrees, jnp.where(valid, lat_index, 0), valid)
    basis_high, basis_low = longitude_basis(by_device.reshape(-1))
    index = me.reshape(1).astype(jnp.int32)
    arrived = []
    outputs = []
    for chunk in range(chunks):
        source = members
        if chunk:
            source, *arrived[chunk - 1] = lax.optimization_barrier((source, *arrived[chunk - 1]))
        arrived.append(exchange(pieces(source, chunk)))
    for chunk in range(chunks):
        parts = arrived[chunk]
        payload = lat_payload(index, parts, target, chunk, high, low, spaces)
        blocks = payload.reshape(groups * spaces, padded, payload.shape[3])
        moved = lax.all_to_all(blocks, ("member", "space"), 0, 0, tiled=True)
        moved = moved.reshape(groups, spaces * padded, payload.shape[3])
        outputs.append(to_longitudes(moved, basis_high, basis_low, local * lanes_of))
    return merge(outputs, local, lats, lanes_of)


def solution(mesh):
    placed = (P("member", None, None, "space", None), P("member", None, "space", None), P())

    return jax.shard_map(
        shards,
        mesh=mesh,
        in_specs=placed,
        out_specs=P("member", None, "space", None),
        check_vma=False,
    )
```

```python
import functools
import math

import jax
import jax.numpy as jnp
from jax import lax
from jax.experimental import pallas as pl
from jax.experimental.pallas import tpu as pltpu
from jax.sharding import PartitionSpec as P


LMAX = 360
NLAT = 361
NLON = 720

EPS = 0.01
LOG_GAMMA_HALF = 0.5 * math.log(math.pi) - math.log(2.0)
STEP_EXP = 64.0
SMALL = 2.0**-64
BIG = 2.0**32
PAD = 8
VMEM_LIMIT = 67_000_000


def round_up(value, multiple):
    return (value + multiple - 1) // multiple * multiple


def split(value):
    high = value.astype(jnp.bfloat16)
    low = (value - high.astype(jnp.float32)).astype(jnp.bfloat16)
    return high, low


def dot(a, b, dims=(((1,), (0,)), ((), ()))):
    return lax.dot_general(a, b, dims, preferred_element_type=jnp.float32)


def table_kernel(step_ref, inv_ref, order_ref, value_ref, scale_ref, cos_ref, high_ref, low_ref, rows_ref):
    group, width = value_ref.shape
    degrees = high_ref.shape[1]
    pitch = degrees + PAD
    order = order_ref[...]
    order_sq = order * order
    cosine = jnp.broadcast_to(cos_ref[0:1, :], (group, width))

    def wide(column):
        return jnp.concatenate([column] * (width // 128), axis=1)

    order_w = wide(order)

    def factors(scale):
        one = jnp.where(scale < -0.5, jnp.where(scale < -2.5, 0.0, SMALL), 1.0)
        two = jnp.where(scale < -1.5, SMALL, 1.0)
        return one, two

    def block(index, carry):
        prev, prev2, scale, root, gap = carry
        big = (jnp.maximum(jnp.abs(prev), jnp.abs(prev2)) > BIG) & (scale < -0.5)
        prev = jnp.where(big, prev * SMALL, prev)
        prev2 = jnp.where(big, prev2 * SMALL, prev2)
        scale = jnp.where(big, scale + 1.0, scale)
        one, two = factors(scale)
        for sub in range(8):
            degree = index * 8 + sub
            deg_f = degree.astype(jnp.float32)
            gap_now = deg_f * deg_f - order_sq
            safe = jnp.maximum(gap_now, 1.0)
            root_now = lax.rsqrt(safe)
            root_now = root_now * (1.5 - 0.5 * safe * root_now * root_now)
            coef_a = step_ref[degree] * root_now
            coef_b = jnp.maximum(gap, 0.0) * root * inv_ref[degree]
            current = wide(coef_a) * (cosine * prev - wide(coef_b) * prev2)
            current = jnp.where(order_w == deg_f, value_ref[...], current)
            shown = (current * one) * two
            for first in range(0, group, 8):
                for lane in range(0, width, 128):
                    rows_ref[lane // 128, pl.ds(first * pitch + degree, 8, pitch), :] = shown[
                        first : first + 8, lane : lane + 128
                    ]
            prev2 = prev
            prev = current
            root, gap = root_now, gap_now
        return prev, prev2, scale, root, gap

    zeros = jnp.zeros((group, width), jnp.float32)
    lax.fori_loop(
        0,
        degrees // 8,
        block,
        (zeros, zeros, scale_ref[...], jnp.ones_like(order), jnp.zeros_like(order)),
    )

    def convert(index, _):
        keep = lax.broadcasted_iota(jnp.int32, (degrees, 128), 0) <= LMAX
        start = pl.multiple_of(index * pitch, 8)
        for tile in range(width // 128):
            value = jnp.where(keep, rows_ref[tile, pl.ds(start, degrees), :], 0.0)
            high, low = split(value)
            lanes = slice(tile * 128, tile * 128 + 128)
            high_ref[index, :, lanes] = high
            low_ref[index, :, lanes] = low
        return 0

    lax.fori_loop(0, group, convert, 0)


def legendre_tables(orders, degrees, lats, valid):
    count = orders.shape[0]
    width = lats.shape[0]
    span = float(NLAT - 1)
    lat_f = lats.astype(jnp.float32)
    nearest = jnp.clip(jnp.minimum(lat_f, span - lat_f), 0.0, None)
    inside = valid & (nearest > 0.0)
    sines = jnp.where(inside, jnp.sin(jnp.pi * nearest / span), 1.0)
    cosines = jnp.cos(jnp.pi * lat_f / span)
    order_f = jnp.minimum(orders, LMAX).astype(jnp.float32)
    log_base = 0.5 * (
        math.log(1.0 / (4.0 * math.pi))
        + lax.lgamma(order_f + 1.5)
        - LOG_GAMMA_HALF
        - lax.lgamma(order_f + 1.0)
    )
    start = (log_base[:, None] + order_f[:, None] * jnp.log(sines)[None, :]) / math.log(2.0)
    scale = jnp.minimum(jnp.floor(start / STEP_EXP + 0.5), 0.0)
    weight = jnp.where(orders > LMAX, 0.0, jnp.where(orders == 0, 1.0, 2.0)).astype(jnp.float32)
    value = jnp.exp2(start - STEP_EXP * scale) * jnp.where(inside, sines, 0.0)[None, :]
    value = value * weight[:, None]
    square = jnp.arange(degrees, dtype=jnp.float32) ** 2
    step = jnp.sqrt(jnp.maximum(4.0 * square - 1.0, 1.0))
    inverse = 1.0 / jnp.concatenate([jnp.ones((1,), jnp.float32), step[:-1]])
    group = 8
    order_cols = jnp.broadcast_to(order_f[:, None], (count, 128))
    cos_rows = jnp.broadcast_to(cosines[None, :], (8, width))
    rows = lambda cols: pl.BlockSpec((group, cols), lambda g, *_: (g, 0))
    out = pl.BlockSpec((group, degrees, width), lambda g, *_: (g, 0, 0))
    shape = jax.ShapeDtypeStruct((count, degrees, width), jnp.bfloat16)
    return pl.pallas_call(
        table_kernel,
        name="legendre_table",
        out_shape=(shape, shape),
        grid_spec=pltpu.PrefetchScalarGridSpec(
            num_scalar_prefetch=2,
            grid=(count // group,),
            in_specs=[rows(128), rows(width), rows(width), pl.BlockSpec((8, width), lambda g, *_: (0, 0))],
            out_specs=(out, out),
            scratch_shapes=[pltpu.VMEM((width // 128, group * (degrees + PAD), 128), jnp.float32)],
        ),
        compiler_params=pltpu.CompilerParams(vmem_limit_bytes=VMEM_LIMIT),
        cost_estimate=pl.CostEstimate(
            flops=10 * count * degrees * width,
            transcendentals=count * degrees,
            bytes_accessed=4 * count * degrees * width,
        ),
    )(step, inverse, order_cols, value, scale, cos_rows)


def cut_kernel(bounds, _, *refs):
    count = len(refs) // (1 + len(bounds))
    for index, source in enumerate(refs[:count]):
        slots = source.shape[0]
        for cut, (first, last) in enumerate(bounds):
            rows = min(last, slots) - first
            for part in range(2):
                refs[count + cut * count + index][part, :rows] = source[first : first + rows, part, :]


def cut_pieces(members, channels, bounds):
    local, _, _, slots, degrees = members.shape
    count = channels.shape[0]
    source = members.transpose(0, 1, 3, 2, 4)

    def in_spec(piece):
        return pl.BlockSpec((None, None, slots, 2, degrees), lambda e, picked: (e, picked[piece], 0, 0, 0))

    shapes = [(2, last - first, degrees) for first, last in bounds for _ in range(count)]
    outs = pl.pallas_call(
        functools.partial(cut_kernel, bounds),
        name="cut_pieces",
        out_shape=[jax.ShapeDtypeStruct((local, *shape), jnp.float32) for shape in shapes],
        grid_spec=pltpu.PrefetchScalarGridSpec(
            num_scalar_prefetch=1,
            grid=(local,),
            in_specs=[in_spec(piece) for piece in range(count)],
            out_specs=[pl.BlockSpec((None, *shape), lambda e, _: (e, 0, 0, 0)) for shape in shapes],
        ),
        compiler_params=pltpu.CompilerParams(vmem_limit_bytes=VMEM_LIMIT),
        cost_estimate=pl.CostEstimate(
            flops=0, transcendentals=0, bytes_accessed=16 * count * local * slots * degrees
        ),
    )(channels, *[source] * count)
    return [outs[cut * count : (cut + 1) * count] for cut in range(len(bounds))]


def gradient_kernel(slots, groups, table_steps, me_ref, *refs):
    blocks = refs[:groups]
    target_ref, band_ref = refs[groups : groups + 2]
    table_refs = refs[groups + 2 : -4]
    out_ref, sums_ref, grads_ref, lat_ref = refs[-4:]
    local = blocks[0].shape[0]
    degrees = target_ref.shape[2]
    width = band_ref.shape[1]
    spaces = out_ref.shape[1]
    width_out = out_ref.shape[3]
    count = groups * local
    rows = 2 * count
    pitch = rows + PAD
    per = 2 * local
    lanes_of = width // spaces
    first_slot = pl.program_id(0) * 8
    live = lax.broadcasted_iota(jnp.int32, (8, 128), 0) + first_slot < slots
    share = 1.0 / count
    pair_share = 1.0 / (count * (count - 1))

    def lane_tile(tile, _):
        lanes = pl.ds(pl.multiple_of(tile * 128, 128), 128)

        def coef(index):
            ref = blocks[index // local]
            return ref[index % local, 0, :, lanes], ref[index % local, 1, :, lanes]

        for group in range(groups):
            base = group * local
            mine = [coef(base + e) for e in range(local)]
            if group == 0:
                total = [[jnp.zeros((8, 128), jnp.float32) for _ in range(2)] for _ in range(local)]
            else:
                total = [[sums_ref[2 * (base + e) + r] for r in range(2)] for e in range(local)]

            def force(a, b):
                real, imag = a[0] - b[0], a[1] - b[1]
                inverse = lax.rsqrt(real * real + (imag * imag + EPS))
                return real * inverse, imag * inverse

            for e in range(local):
                for f in range(e + 1, local):
                    pull = force(mine[e], mine[f])
                    for r in range(2):
                        total[e][r] = total[e][r] + pull[r]
                        total[f][r] = total[f][r] - pull[r]
            for other in range(base + local, count):
                theirs = coef(other)
                sums = None if group == 0 else [sums_ref[2 * other + r] for r in range(2)]
                for e in range(local):
                    pull = force(mine[e], theirs)
                    for r in range(2):
                        total[e][r] = total[e][r] + pull[r]
                    if sums is None:
                        sums = [-pull[0], -pull[1]]
                    else:
                        sums = [sums[0] - pull[0], sums[1] - pull[1]]
                for r in range(2):
                    sums_ref[2 * other + r] = sums[r]
            goal = (target_ref[0, :, lanes], target_ref[1, :, lanes])
            owner = lax.rem(me_ref[0] + (groups - group), groups)
            for e in range(local):
                pull = force(mine[e], goal)
                for r in range(2):
                    grad = pull[r] * share - total[e][r] * pair_share
                    grad = jnp.where(live, grad, 0.0)
                    grads_ref[tile, pl.ds(owner * per + r * local + e, 8, pitch), :] = grad
        return 0

    lax.fori_loop(0, degrees // 128, lane_tile, 0)

    def transform(high_ref, low_ref):
        def one(slot, _):
            start = pl.multiple_of(slot * pitch, 8)
            grad = jnp.concatenate(
                [grads_ref[tile, pl.ds(start, rows), :] for tile in range(degrees // 128)], axis=1
            )
            high, low = split(grad)
            both = dot(jnp.concatenate([high, low], axis=0), high_ref[slot])
            lat = both[:rows] + both[rows:] + dot(high, low_ref[slot])
            for tile in range(width // 128):
                lat_ref[tile, pl.ds(start, rows), :] = lat[:, tile * 128 : tile * 128 + 128]
            return 0

        lax.fori_loop(0, 8, one, 0, unroll=8 if len(table_steps) == 1 else 4)

    if len(table_steps) == 1:
        transform(*table_refs)
    else:
        first = 0
        for index, steps in enumerate(table_steps):
            here = (pl.program_id(0) >= first) & (pl.program_id(0) < first + steps)
            pl.when(here)(functools.partial(transform, *table_refs[2 * index : 2 * index + 2]))
            first += steps

    band = band_ref[...]

    def load(group, row):
        parts = [
            lat_ref[tile, pl.ds(group * per + row, 8, pitch), :] for tile in range(width // 128)
        ]
        return jnp.concatenate(parts, axis=1)

    def scatter(group, _):
        source = [load(group, row) for row in range(per)]
        if spaces == per and width == width_out:
            distance = per // 2
            while distance:
                upper = (band & distance) != 0
                for i in range(per):
                    if i & distance:
                        continue
                    j = i | distance
                    shift = distance * lanes_of
                    from_j = pltpu.roll(source[j], shift, 1)
                    from_i = pltpu.roll(source[i], width - shift, 1)
                    source[i], source[j] = (
                        jnp.where(upper, from_j, source[i]),
                        jnp.where(upper, source[j], from_i),
                    )
                distance //= 2
            for space in range(spaces):
                out_ref[group, space] = source[space]
        else:
            for space in range(spaces):
                value = jnp.zeros((8, width_out), jnp.float32)
                for row in range(per):
                    shift = (row - space) * lanes_of % width
                    moved = source[row] if shift == 0 else pltpu.roll(source[row], shift, 1)
                    value = jnp.where(band[:, :width_out] == row, moved[:, :width_out], value)
                out_ref[group, space] = value
        return 0

    lax.fori_loop(0, groups, scatter, 0)


def lat_payload(me, slots, parts, targets, channel, first_step, tables, spaces):
    local, _, _, degrees = parts[0].shape
    groups = len(parts)
    width = tables[0][0].shape[2]
    steps = [high.shape[0] // 8 for high, _ in tables]
    padded = 8 * sum(steps)
    per = 2 * local
    lanes_of = width // spaces
    width_out = round_up(per * lanes_of, 128)
    count = groups * local
    band = jnp.broadcast_to((jnp.arange(width, dtype=jnp.int32) // lanes_of)[None], (8, width))
    part_spec = pl.BlockSpec((local, 2, 8, degrees), lambda g, *_: (0, 0, g, 0))
    table_specs = []
    before = 0
    for size in steps:
        index = lambda g, *_, size=size, before=before: (jnp.clip(g - before, 0, size - 1), 0, 0)
        table_specs += [pl.BlockSpec((8, degrees, width), index)] * 2
        before += size
    pairs = count * (count + 1) // 2
    return pl.pallas_call(
        functools.partial(gradient_kernel, slots, groups, tuple(steps)),
        name="loss_gradient",
        out_shape=jax.ShapeDtypeStruct((groups, spaces, padded, width_out), jnp.float32),
        grid_spec=pltpu.PrefetchScalarGridSpec(
            num_scalar_prefetch=1,
            grid=(padded // 8,),
            in_specs=[part_spec] * groups
            + [
                pl.BlockSpec((None, 2, 8, degrees), lambda g, *_: (channel, 0, g + first_step, 0)),
                pl.BlockSpec((8, width), lambda g, *_: (0, 0)),
            ]
            + table_specs,
            out_specs=pl.BlockSpec((groups, spaces, 8, width_out), lambda g, *_: (0, 0, g, 0)),
            scratch_shapes=[
                pltpu.VMEM((2 * count, 8, 128), jnp.float32),
                pltpu.VMEM((degrees // 128, 8 * (2 * count + PAD), 128), jnp.float32),
                pltpu.VMEM((width // 128, 8 * (2 * count + PAD), 128), jnp.float32),
            ],
        ),
        compiler_params=pltpu.CompilerParams(vmem_limit_bytes=VMEM_LIMIT),
        cost_estimate=pl.CostEstimate(
            flops=6 * 2 * count * padded * degrees * width,
            transcendentals=pairs * padded * degrees,
            bytes_accessed=4 * padded * degrees * width + 16 * count * padded * degrees,
        ),
    )(me, *parts, targets, band, *[array for pair in tables for array in pair])


def longitude_kernel(count, *refs):
    out_ref = refs[-1]
    half = out_ref.shape[0]
    total = None
    for index in range(count):
        value = refs[index][...].T
        both = jnp.concatenate([value[:half], value[half : 2 * half]], axis=1)
        high, low = split(both)
        basis_high, basis_low = refs[count + 2 * index][...], refs[count + 2 * index + 1][...]
        part = dot(high, basis_high) + dot(low, basis_high) + dot(high, basis_low)
        total = part if total is None else total + part
    out_ref[...] = total


def to_longitudes(received, bases, half):
    groups, _, width = received[0].shape
    whole = lambda array: pl.BlockSpec(array.shape, lambda g: (0, 0))
    flat = [array for pair in bases for array in pair]
    depth = sum(array.shape[1] for array in received)
    return pl.pallas_call(
        functools.partial(longitude_kernel, len(received)),
        name="longitudes",
        out_shape=jax.ShapeDtypeStruct((groups, half, NLON), jnp.float32),
        grid=(groups,),
        in_specs=[pl.BlockSpec((None, *array.shape[1:]), lambda g: (g, 0, 0)) for array in received]
        + [whole(array) for array in flat],
        out_specs=pl.BlockSpec((None, half, NLON), lambda g: (g, 0, 0)),
        compiler_params=pltpu.CompilerParams(vmem_limit_bytes=VMEM_LIMIT),
        cost_estimate=pl.CostEstimate(
            flops=6 * groups * half * 2 * depth * NLON,
            transcendentals=0,
            bytes_accessed=4 * groups * (depth * width + half * NLON),
        ),
    )(*received, *flat)


def merge_kernel(lats, lanes_of, got_ref, high_ref, low_ref, *refs):
    ins, (out_ref, turned_ref, wide_ref) = refs[:-3], refs[-3:]
    groups, _, _ = got_ref.shape
    chunks = len(ins) + 1
    channels = groups * chunks
    local = pl.num_programs(0)
    spread = round_up(lanes_of, 8)
    pitch = channels + PAD
    member = pl.program_id(0)

    @pl.when(member == 0)
    def _():
        for group in range(groups):
            turned = got_ref[group].T
            for piece in range(turned_ref.shape[1] // spread):
                turned_ref[group, piece * spread : piece * spread + lanes_of, :] = turned[
                    piece * lanes_of : (piece + 1) * lanes_of
                ]

    def part(group, side):
        start = pl.multiple_of((side * local + member) * spread, 8)
        return turned_ref[group, pl.ds(start, lanes_of), :]

    rows = [jnp.concatenate([part(group, 0), part(group, 1)], axis=1) for group in range(groups)]
    high, low = split(jnp.concatenate(rows, axis=0))
    last = dot(high, high_ref[...]) + dot(low, high_ref[...]) + dot(high, low_ref[...])

    def place(value, channel, first, lane):
        rows, size = value.shape
        if size < 128:
            value = jnp.concatenate([value, jnp.zeros((rows, 128 - size), jnp.float32)], axis=1)
        wide_ref[lane // 128, pl.ds(first * pitch + channel, rows, pitch), :] = value

    for lane in range(0, NLON, 128):
        size = min(128, NLON - lane)
        for group in range(groups):
            for first in range(0, lanes_of, 8):
                rows = min(8, lanes_of - first)
                for chunk in range(chunks - 1):
                    value = ins[chunk][group, pl.ds(first, rows), lane : lane + size]
                    place(value, group * chunks + chunk, first, lane)
                value = last[group * lanes_of + first :, lane : lane + size][:rows]
                place(value, group * chunks + chunks - 1, first, lane)
        for lat in range(lats):
            out_ref[lat * channels : (lat + 1) * channels, lane : lane + size] = wide_ref[
                lane // 128, lat * pitch : lat * pitch + channels, :size
            ]


def merge(received, high, low, parts, local, lats, lanes_of):
    groups, depth, _ = received.shape
    channels = groups * (len(parts) + 1)
    parts = [part.reshape(groups, local, lanes_of, NLON) for part in parts]
    out = pl.pallas_call(
        functools.partial(merge_kernel, lats, lanes_of),
        name="merge_channels",
        out_shape=jax.ShapeDtypeStruct((local, lats * channels, NLON), jnp.float32),
        grid=(local,),
        in_specs=[
            pl.BlockSpec(received.shape, lambda e: (0, 0, 0)),
            pl.BlockSpec(high.shape, lambda e: (0, 0)),
            pl.BlockSpec(low.shape, lambda e: (0, 0)),
        ]
        + [pl.BlockSpec((groups, None, lanes_of, NLON), lambda e: (0, e, 0, 0))] * len(parts),
        out_specs=pl.BlockSpec((None, lats * channels, NLON), lambda e: (e, 0, 0)),
        scratch_shapes=[
            pltpu.VMEM((groups, 2 * local * round_up(lanes_of, 8), depth), jnp.float32),
            pltpu.VMEM((pl.cdiv(NLON, 128), lanes_of * (channels + PAD), 128), jnp.float32),
        ],
        compiler_params=pltpu.CompilerParams(vmem_limit_bytes=VMEM_LIMIT),
        cost_estimate=pl.CostEstimate(
            flops=6 * local * groups * lanes_of * 2 * depth * NLON,
            transcendentals=0,
            bytes_accessed=8 * local * lats * channels * NLON,
        ),
    )(received, high, low, *parts)
    return out.reshape(local, lats, channels, NLON).transpose(0, 2, 1, 3)


def longitude_basis(orders):
    cols = jnp.arange(NLON, dtype=jnp.int32)
    phase = orders[:, None] * cols[None, :] % NLON
    angle = 2.0 * jnp.pi * phase.astype(jnp.float32) / NLON
    valid = (orders <= LMAX)[:, None]
    scale = 2.0 * jnp.pi / NLON
    cosine = jnp.where(valid, jnp.cos(angle), 0.0) * scale
    sine = jnp.where(valid, -jnp.sin(angle), 0.0) * scale
    value = jnp.concatenate([cosine, sine], axis=0)
    high = lax.reduce_precision(value, 8, 7)
    return high.astype(jnp.bfloat16), (value - high).astype(jnp.bfloat16)


def shards(members, target, order_table):
    local, channels, _, slots, degrees = members.shape
    spaces = lax.axis_size("space")
    groups = lax.axis_size("member")
    chunks = channels // groups
    me = lax.axis_index("member")
    padded = round_up(slots, 16)
    lats = (NLAT + spaces - 1) // spaces
    width = round_up(spaces * lats, 128)
    lanes_of = width // spaces

    by_device = jnp.pad(
        order_table.reshape(spaces, slots), ((0, 0), (0, padded - slots)), constant_values=LMAX + 1
    )
    mine = lax.dynamic_index_in_dim(by_device, lax.axis_index("space"), 0, keepdims=False)
    column = jnp.arange(width, dtype=jnp.int32)
    inner = column % lanes_of
    lat_index = column // lanes_of * lats + inner
    valid = (inner < lats) & (lat_index < NLAT)

    def pieces(source, chunk, bounds):
        picked = lax.rem(me + jnp.arange(groups, dtype=jnp.int32), groups) * chunks + chunk
        return cut_pieces(source, picked.astype(jnp.int32), bounds)

    def exchange(cut):
        return [cut[0]] + [
            lax.ppermute(cut[step], "member", [(i, (i + step) % groups) for i in range(groups)])
            for step in range(1, groups)
        ]

    lat_rows = jnp.where(valid, lat_index, 0)
    head = round_up(padded // 2, 8)
    items = [(0, 0, head), (0, head, padded)] + [(chunk, 0, padded) for chunk in range(1, chunks)]
    index = me.reshape(1).astype(jnp.int32)

    arrived = []
    early = pieces(members, 0, [item[1:] for item in items[:2]])
    for cut in early:
        arrived.append(exchange(cut))
    for number, (chunk, first, last) in enumerate(items[2:], 2):
        source, *arrived[-1] = lax.optimization_barrier((members, *arrived[-1]))
        arrived.append(exchange(pieces(source, chunk, [(first, last)])[0]))

    tables = {}
    received = []
    for number, (chunk, first, last) in enumerate(items):
        if number < 2:
            tables[number] = legendre_tables(mine[first:last], degrees, lat_rows, valid)
        used = [tables[number]] if number < 2 else [tables[0], tables[1]]
        count = min(last, slots) - first
        payload = lat_payload(
            index, count, arrived[number], target, chunk, first // 8, used, spaces
        )
        if number == 0:
            payload, mine = lax.optimization_barrier((payload, mine))
        blocks = payload.reshape(groups * spaces, last - first, payload.shape[3])
        moved = lax.all_to_all(blocks, ("member", "space"), 0, 0, tiled=True)
        received.append(moved.reshape(groups, spaces * (last - first), payload.shape[3]))

    bases = [
        longitude_basis(by_device[:, first:last].reshape(-1)) for _, first, last in items[:2]
    ]
    full = longitude_basis(by_device.reshape(-1))
    half = local * lanes_of
    outputs = [to_longitudes(received[:2], bases, half)]
    outputs += [to_longitudes([got], [full], half) for got in received[2:-1]]
    return merge(received[-1], *full, outputs, local, lats, lanes_of)


def solution(mesh):
    placed = (P("member", None, None, "space", None), P("member", None, "space", None), P())

    return jax.shard_map(
        shards,
        mesh=mesh,
        in_specs=placed,
        out_specs=P("member", None, "space", None),
        check_vma=False,
    )
```

```python
import functools
import math

import jax
import jax.numpy as jnp
from jax import lax
from jax.experimental import pallas as pl
from jax.experimental.pallas import tpu as pltpu
from jax.sharding import PartitionSpec as P


LMAX = 360
NLAT = 361
NLON = 720

EPS = 0.01
LOG_GAMMA_HALF = 0.5 * math.log(math.pi) - math.log(2.0)
STEP_EXP = 64.0
SMALL = 2.0**-64
BIG = 2.0**32
PAD = 8
VMEM_LIMIT = 67_000_000


def round_up(value, multiple):
    return (value + multiple - 1) // multiple * multiple


def split(value):
    high = value.astype(jnp.bfloat16)
    low = (value - high.astype(jnp.float32)).astype(jnp.bfloat16)
    return high, low


def dot(a, b, dims=(((1,), (0,)), ((), ()))):
    return lax.dot_general(a, b, dims, preferred_element_type=jnp.float32)


def table_kernel(step_ref, inv_ref, order_ref, value_ref, scale_ref, cos_ref, high_ref, low_ref, rows_ref):
    group, width = value_ref.shape
    degrees = high_ref.shape[1]
    pitch = degrees + PAD
    order = order_ref[...]
    order_sq = order * order
    cosine = jnp.broadcast_to(cos_ref[0:1, :], (group, width))

    def wide(column):
        return jnp.concatenate([column] * (width // 128), axis=1)

    order_w = wide(order)

    def factors(scale):
        one = jnp.where(scale < -0.5, jnp.where(scale < -2.5, 0.0, SMALL), 1.0)
        two = jnp.where(scale < -1.5, SMALL, 1.0)
        return one, two

    def block(index, carry):
        prev, prev2, scale, root, gap = carry
        big = (jnp.maximum(jnp.abs(prev), jnp.abs(prev2)) > BIG) & (scale < -0.5)
        prev = jnp.where(big, prev * SMALL, prev)
        prev2 = jnp.where(big, prev2 * SMALL, prev2)
        scale = jnp.where(big, scale + 1.0, scale)
        one, two = factors(scale)
        for sub in range(8):
            degree = index * 8 + sub
            deg_f = degree.astype(jnp.float32)
            gap_now = deg_f * deg_f - order_sq
            root_now = lax.rsqrt(jnp.maximum(gap_now, 1.0))
            coef_a = step_ref[degree] * root_now
            coef_b = jnp.maximum(gap, 0.0) * root * inv_ref[degree]
            current = wide(coef_a) * (cosine * prev - wide(coef_b) * prev2)
            current = jnp.where(order_w == deg_f, value_ref[...], current)
            shown = (current * one) * two
            for first in range(0, group, 8):
                for lane in range(0, width, 128):
                    rows_ref[lane // 128, pl.ds(first * pitch + degree, 8, pitch), :] = shown[
                        first : first + 8, lane : lane + 128
                    ]
            prev2 = prev
            prev = current
            root, gap = root_now, gap_now
        return prev, prev2, scale, root, gap

    zeros = jnp.zeros((group, width), jnp.float32)
    lax.fori_loop(
        0,
        degrees // 8,
        block,
        (zeros, zeros, scale_ref[...], jnp.ones_like(order), jnp.zeros_like(order)),
    )

    def convert(index, _):
        keep = lax.broadcasted_iota(jnp.int32, (degrees, 128), 0) <= LMAX
        start = pl.multiple_of(index * pitch, 8)
        for tile in range(width // 128):
            value = jnp.where(keep, rows_ref[tile, pl.ds(start, degrees), :], 0.0)
            high, low = split(value)
            lanes = slice(tile * 128, tile * 128 + 128)
            high_ref[index, :, lanes] = high
            low_ref[index, :, lanes] = low
        return 0

    lax.fori_loop(0, group, convert, 0)


def table_inputs(orders, degrees, lats, valid):
    count = orders.shape[0]
    width = lats.shape[0]
    span = float(NLAT - 1)
    lat_f = lats.astype(jnp.float32)
    nearest = jnp.clip(jnp.minimum(lat_f, span - lat_f), 0.0, None)
    inside = valid & (nearest > 0.0)
    sines = jnp.where(inside, jnp.sin(jnp.pi * nearest / span), 1.0)
    cosines = jnp.cos(jnp.pi * lat_f / span)
    order_f = jnp.minimum(orders, LMAX).astype(jnp.float32)
    log_base = 0.5 * (
        math.log(1.0 / (4.0 * math.pi))
        + lax.lgamma(order_f + 1.5)
        - LOG_GAMMA_HALF
        - lax.lgamma(order_f + 1.0)
    )
    start = (log_base[:, None] + order_f[:, None] * jnp.log(sines)[None, :]) / math.log(2.0)
    scale = jnp.minimum(jnp.floor(start / STEP_EXP + 0.5), 0.0)
    weight = jnp.where(orders > LMAX, 0.0, jnp.where(orders == 0, 1.0, 2.0)).astype(jnp.float32)
    value = jnp.exp2(start - STEP_EXP * scale) * jnp.where(inside, sines, 0.0)[None, :]
    value = value * weight[:, None]
    square = jnp.arange(degrees, dtype=jnp.float32) ** 2
    step = jnp.sqrt(jnp.maximum(4.0 * square - 1.0, 1.0))
    inverse = 1.0 / jnp.concatenate([jnp.ones((1,), jnp.float32), step[:-1]])
    order_cols = jnp.broadcast_to(order_f[:, None], (count, 128))
    cos_rows = jnp.broadcast_to(cosines[None, :], (8, width))
    return step, inverse, order_cols, value, scale, cos_rows


def legendre_tables(orders, degrees, lats, valid):
    step, inverse, order_cols, value, scale, cos_rows = table_inputs(orders, degrees, lats, valid)
    count, width = value.shape
    group = 8
    rows = lambda cols: pl.BlockSpec((group, cols), lambda g, *_: (g, 0))
    out = pl.BlockSpec((group, degrees, width), lambda g, *_: (g, 0, 0))
    shape = jax.ShapeDtypeStruct((count, degrees, width), jnp.bfloat16)
    return pl.pallas_call(
        table_kernel,
        name="legendre_table",
        out_shape=(shape, shape),
        grid_spec=pltpu.PrefetchScalarGridSpec(
            num_scalar_prefetch=2,
            grid=(count // group,),
            in_specs=[rows(128), rows(width), rows(width), pl.BlockSpec((8, width), lambda g, *_: (0, 0))],
            out_specs=(out, out),
            scratch_shapes=[pltpu.VMEM((width // 128, group * (degrees + PAD), 128), jnp.float32)],
        ),
        compiler_params=pltpu.CompilerParams(vmem_limit_bytes=VMEM_LIMIT),
        cost_estimate=pl.CostEstimate(
            flops=10 * count * degrees * width,
            transcendentals=count * degrees,
            bytes_accessed=4 * count * degrees * width,
        ),
    )(step, inverse, order_cols, value, scale, cos_rows)


def cut_kernel(bounds, _, *refs):
    count = len(refs) // (1 + len(bounds))
    for index, source in enumerate(refs[:count]):
        slots = source.shape[0]
        for cut, (first, last) in enumerate(bounds):
            rows = min(last, slots) - first
            for part in range(2):
                refs[count + cut * count + index][part, :rows] = source[first : first + rows, part, :]


def cut_pieces(members, channels, bounds):
    local, _, _, slots, degrees = members.shape
    count = channels.shape[0]
    source = members.transpose(0, 1, 3, 2, 4)

    def in_spec(piece):
        return pl.BlockSpec((None, None, slots, 2, degrees), lambda e, picked: (e, picked[piece], 0, 0, 0))

    shapes = [(2, last - first, degrees) for first, last in bounds for _ in range(count)]
    outs = pl.pallas_call(
        functools.partial(cut_kernel, bounds),
        name="cut_pieces",
        out_shape=[jax.ShapeDtypeStruct((local, *shape), jnp.float32) for shape in shapes],
        grid_spec=pltpu.PrefetchScalarGridSpec(
            num_scalar_prefetch=1,
            grid=(local,),
            in_specs=[in_spec(piece) for piece in range(count)],
            out_specs=[pl.BlockSpec((None, *shape), lambda e, _: (e, 0, 0, 0)) for shape in shapes],
        ),
        compiler_params=pltpu.CompilerParams(vmem_limit_bytes=VMEM_LIMIT),
        cost_estimate=pl.CostEstimate(
            flops=0, transcendentals=0, bytes_accessed=16 * count * local * slots * degrees
        ),
    )(channels, *[source] * count)
    return [outs[cut * count : (cut + 1) * count] for cut in range(len(bounds))]


def gradient_kernel(slots, groups, table_steps, me_ref, *refs):
    blocks = refs[:groups]
    target_ref, band_ref = refs[groups : groups + 2]
    table_refs = refs[groups + 2 : -4]
    out_ref, sums_ref, grads_ref, lat_ref = refs[-4:]
    local = blocks[0].shape[0]
    degrees = target_ref.shape[2]
    width = band_ref.shape[1]
    spaces = out_ref.shape[1]
    width_out = out_ref.shape[3]
    count = groups * local
    rows = 2 * count
    pitch = rows + PAD
    per = 2 * local
    lanes_of = width // spaces
    first_slot = pl.program_id(0) * 8
    live = lax.broadcasted_iota(jnp.int32, (8, 128), 0) + first_slot < slots
    share = 1.0 / count
    pair_share = 1.0 / (count * (count - 1))

    def lane_tile(tile, _):
        lanes = pl.ds(pl.multiple_of(tile * 128, 128), 128)

        def coef(index):
            ref = blocks[index // local]
            return ref[index % local, 0, :, lanes], ref[index % local, 1, :, lanes]

        for group in range(groups):
            base = group * local
            mine = [coef(base + e) for e in range(local)]
            if group == 0:
                total = [[jnp.zeros((8, 128), jnp.float32) for _ in range(2)] for _ in range(local)]
            else:
                total = [[sums_ref[2 * (base + e) + r] for r in range(2)] for e in range(local)]

            def force(a, b):
                real, imag = a[0] - b[0], a[1] - b[1]
                inverse = lax.rsqrt(real * real + (imag * imag + EPS))
                return real * inverse, imag * inverse

            for e in range(local):
                for f in range(e + 1, local):
                    pull = force(mine[e], mine[f])
                    for r in range(2):
                        total[e][r] = total[e][r] + pull[r]
                        total[f][r] = total[f][r] - pull[r]
            for other in range(base + local, count):
                theirs = coef(other)
                sums = None if group == 0 else [sums_ref[2 * other + r] for r in range(2)]
                for e in range(local):
                    pull = force(mine[e], theirs)
                    for r in range(2):
                        total[e][r] = total[e][r] + pull[r]
                    if sums is None:
                        sums = [-pull[0], -pull[1]]
                    else:
                        sums = [sums[0] - pull[0], sums[1] - pull[1]]
                for r in range(2):
                    sums_ref[2 * other + r] = sums[r]
            goal = (target_ref[:, 0, lanes], target_ref[:, 1, lanes])
            owner = lax.rem(me_ref[0] + (groups - group), groups)
            for e in range(local):
                pull = force(mine[e], goal)
                for r in range(2):
                    grad = pull[r] * share - total[e][r] * pair_share
                    grad = jnp.where(live, grad, 0.0)
                    grads_ref[tile, pl.ds(owner * per + r * local + e, 8, pitch), :] = grad
        return 0

    lax.fori_loop(0, degrees // 128, lane_tile, 0)

    def transform(high_ref, low_ref):
        def one(slot, _):
            start = pl.multiple_of(slot * pitch, 8)
            grad = jnp.concatenate(
                [grads_ref[tile, pl.ds(start, rows), :] for tile in range(degrees // 128)], axis=1
            )
            high, low = split(grad)
            both = dot(jnp.concatenate([high, low], axis=0), high_ref[slot])
            lat = both[:rows] + both[rows:] + dot(high, low_ref[slot])
            for tile in range(width // 128):
                lat_ref[tile, pl.ds(start, rows), :] = lat[:, tile * 128 : tile * 128 + 128]
            return 0

        lax.fori_loop(0, 8, one, 0, unroll=8 if len(table_steps) == 1 else 4)

    if len(table_steps) == 1:
        transform(*table_refs)
    else:
        first = 0
        for index, steps in enumerate(table_steps):
            here = (pl.program_id(0) >= first) & (pl.program_id(0) < first + steps)
            pl.when(here)(functools.partial(transform, *table_refs[2 * index : 2 * index + 2]))
            first += steps

    band = band_ref[...]

    def load(group, row):
        parts = [
            lat_ref[tile, pl.ds(group * per + row, 8, pitch), :] for tile in range(width // 128)
        ]
        return jnp.concatenate(parts, axis=1)

    def scatter(group, _):
        source = [load(group, row) for row in range(per)]
        if spaces == per and width == width_out:
            distance = per // 2
            while distance:
                upper = (band & distance) != 0
                for i in range(per):
                    if i & distance:
                        continue
                    j = i | distance
                    shift = distance * lanes_of
                    from_j = pltpu.roll(source[j], shift, 1)
                    from_i = pltpu.roll(source[i], width - shift, 1)
                    source[i], source[j] = (
                        jnp.where(upper, from_j, source[i]),
                        jnp.where(upper, source[j], from_i),
                    )
                distance //= 2
            for space in range(spaces):
                out_ref[group, space] = source[space]
        else:
            for space in range(spaces):
                value = jnp.zeros((8, width_out), jnp.float32)
                for row in range(per):
                    shift = (row - space) * lanes_of % width
                    moved = source[row] if shift == 0 else pltpu.roll(source[row], shift, 1)
                    value = jnp.where(band[:, :width_out] == row, moved[:, :width_out], value)
                out_ref[group, space] = value
        return 0

    lax.fori_loop(0, groups, scatter, 0)


def fused_kernel(slots, groups, me_ref, step_ref, inv_ref, *refs):
    blocks, rest = refs[:groups], refs[groups:]
    target_ref, band_ref, order_ref, value_ref, scale_ref, cos_ref = rest[:6]
    out_ref, high_ref, low_ref, sums_ref, grads_ref, lat_ref, rows_ref = rest[6:]
    table_kernel(
        step_ref, inv_ref, order_ref, value_ref, scale_ref, cos_ref, high_ref, low_ref, rows_ref
    )
    gradient_kernel(
        slots, groups, (1,), me_ref, *blocks, target_ref, band_ref, high_ref, low_ref,
        out_ref, sums_ref, grads_ref, lat_ref,
    )


def lat_payload(me, slots, parts, targets, channel, first_step, tables, spaces, build=None):
    local, _, _, degrees = parts[0].shape
    groups = len(parts)
    if build is None:
        width = tables[0][0].shape[2]
        steps = [high.shape[0] // 8 for high, _ in tables]
    else:
        count_rows, width = build[3].shape
        steps = [count_rows // 8]
    padded = 8 * sum(steps)
    per = 2 * local
    lanes_of = width // spaces
    width_out = round_up(per * lanes_of, 128)
    count = groups * local
    band = jnp.broadcast_to((jnp.arange(width, dtype=jnp.int32) // lanes_of)[None], (8, width))
    part_spec = pl.BlockSpec((local, 2, 8, degrees), lambda g, *_: (0, 0, g, 0))
    in_specs = [part_spec] * groups + [
        pl.BlockSpec((None, 8, 2, degrees), lambda g, *_: (channel, g + first_step, 0, 0)),
        pl.BlockSpec((8, width), lambda g, *_: (0, 0)),
    ]
    out_shape = [jax.ShapeDtypeStruct((groups, spaces, padded, width_out), jnp.float32)]
    out_specs = [pl.BlockSpec((groups, spaces, 8, width_out), lambda g, *_: (0, 0, g, 0))]
    scratch = [
        pltpu.VMEM((2 * count, 8, 128), jnp.float32),
        pltpu.VMEM((degrees // 128, 8 * (2 * count + PAD), 128), jnp.float32),
        pltpu.VMEM((width // 128, 8 * (2 * count + PAD), 128), jnp.float32),
    ]
    scalars = (me,)
    if build is None:
        kernel = functools.partial(gradient_kernel, slots, groups, tuple(steps))
        before = 0
        for size in steps:
            index = lambda g, *_, size=size, before=before: (jnp.clip(g - before, 0, size - 1), 0, 0)
            in_specs += [pl.BlockSpec((8, degrees, width), index)] * 2
            before += size
        extra = [array for pair in tables for array in pair]
    else:
        kernel = functools.partial(fused_kernel, slots, groups)
        scalars += build[:2]
        extra = list(build[2:])
        rows = lambda cols: pl.BlockSpec((8, cols), lambda g, *_: (g, 0))
        in_specs += [rows(128), rows(width), rows(width), pl.BlockSpec((8, width), lambda g, *_: (0, 0))]
        out_shape += [jax.ShapeDtypeStruct((padded, degrees, width), jnp.bfloat16)] * 2
        out_specs += [pl.BlockSpec((8, degrees, width), lambda g, *_: (g, 0, 0))] * 2
        scratch.append(pltpu.VMEM((width // 128, 8 * (degrees + PAD), 128), jnp.float32))
    pairs = count * (count + 1) // 2
    outs = pl.pallas_call(
        kernel,
        name="loss_gradient",
        out_shape=out_shape,
        grid_spec=pltpu.PrefetchScalarGridSpec(
            num_scalar_prefetch=len(scalars),
            grid=(padded // 8,),
            in_specs=in_specs,
            out_specs=out_specs,
            scratch_shapes=scratch,
        ),
        compiler_params=pltpu.CompilerParams(vmem_limit_bytes=VMEM_LIMIT),
        cost_estimate=pl.CostEstimate(
            flops=6 * 2 * count * padded * degrees * width,
            transcendentals=pairs * padded * degrees,
            bytes_accessed=4 * padded * degrees * width + 16 * count * padded * degrees,
        ),
    )(*scalars, *parts, targets.transpose(0, 2, 1, 3), band, *extra)
    return outs[0] if build is None else (outs[0], (outs[1], outs[2]))


def longitude_kernel(count, *refs):
    out_ref = refs[-1]
    half = out_ref.shape[0]
    total = None
    for index in range(count):
        value = refs[index][...].T
        both = jnp.concatenate([value[:half], value[half : 2 * half]], axis=1)
        high, low = split(both)
        basis_high, basis_low = refs[count + 2 * index][...], refs[count + 2 * index + 1][...]
        part = dot(high, basis_high) + dot(low, basis_high) + dot(high, basis_low)
        total = part if total is None else total + part
    out_ref[...] = total


def to_longitudes(received, bases, half):
    groups, _, width = received[0].shape
    whole = lambda array: pl.BlockSpec(array.shape, lambda g: (0, 0))
    flat = [array for pair in bases for array in pair]
    depth = sum(array.shape[1] for array in received)
    return pl.pallas_call(
        functools.partial(longitude_kernel, len(received)),
        name="longitudes",
        out_shape=jax.ShapeDtypeStruct((groups, half, NLON), jnp.float32),
        grid=(groups,),
        in_specs=[pl.BlockSpec((None, *array.shape[1:]), lambda g: (g, 0, 0)) for array in received]
        + [whole(array) for array in flat],
        out_specs=pl.BlockSpec((None, half, NLON), lambda g: (g, 0, 0)),
        compiler_params=pltpu.CompilerParams(vmem_limit_bytes=VMEM_LIMIT),
        cost_estimate=pl.CostEstimate(
            flops=6 * groups * half * 2 * depth * NLON,
            transcendentals=0,
            bytes_accessed=4 * groups * (depth * width + half * NLON),
        ),
    )(*received, *flat)


def merge_kernel(lats, lanes_of, got_ref, high_ref, low_ref, *refs):
    ins, (out_ref, turned_ref, wide_ref) = refs[:-3], refs[-3:]
    groups, _, _ = got_ref.shape
    chunks = len(ins) + 1
    channels = groups * chunks
    local = pl.num_programs(0)
    spread = round_up(lanes_of, 8)
    pitch = channels + PAD
    member = pl.program_id(0)

    @pl.when(member == 0)
    def _():
        for group in range(groups):
            turned = got_ref[group].T
            for piece in range(turned_ref.shape[1] // spread):
                turned_ref[group, piece * spread : piece * spread + lanes_of, :] = turned[
                    piece * lanes_of : (piece + 1) * lanes_of
                ]

    def part(group, side):
        start = pl.multiple_of((side * local + member) * spread, 8)
        return turned_ref[group, pl.ds(start, lanes_of), :]

    rows = [jnp.concatenate([part(group, 0), part(group, 1)], axis=1) for group in range(groups)]
    high, low = split(jnp.concatenate(rows, axis=0))
    last = dot(high, high_ref[...]) + dot(low, high_ref[...]) + dot(high, low_ref[...])

    def place(value, channel, first, lane):
        rows, size = value.shape
        if size < 128:
            value = jnp.concatenate([value, jnp.zeros((rows, 128 - size), jnp.float32)], axis=1)
        wide_ref[lane // 128, pl.ds(first * pitch + channel, rows, pitch), :] = value

    for lane in range(0, NLON, 128):
        size = min(128, NLON - lane)
        for group in range(groups):
            for first in range(0, lanes_of, 8):
                rows = min(8, lanes_of - first)
                for chunk in range(chunks - 1):
                    value = ins[chunk][group, pl.ds(first, rows), lane : lane + size]
                    place(value, group * chunks + chunk, first, lane)
                value = last[group * lanes_of + first :, lane : lane + size][:rows]
                place(value, group * chunks + chunks - 1, first, lane)
        for lat in range(lats):
            out_ref[lat * channels : (lat + 1) * channels, lane : lane + size] = wide_ref[
                lane // 128, lat * pitch : lat * pitch + channels, :size
            ]


def merge(received, high, low, parts, local, lats, lanes_of):
    groups, depth, _ = received.shape
    channels = groups * (len(parts) + 1)
    parts = [part.reshape(groups, local, lanes_of, NLON) for part in parts]
    out = pl.pallas_call(
        functools.partial(merge_kernel, lats, lanes_of),
        name="merge_channels",
        out_shape=jax.ShapeDtypeStruct((local, lats * channels, NLON), jnp.float32),
        grid=(local,),
        in_specs=[
            pl.BlockSpec(received.shape, lambda e: (0, 0, 0)),
            pl.BlockSpec(high.shape, lambda e: (0, 0)),
            pl.BlockSpec(low.shape, lambda e: (0, 0)),
        ]
        + [pl.BlockSpec((groups, None, lanes_of, NLON), lambda e: (0, e, 0, 0))] * len(parts),
        out_specs=pl.BlockSpec((None, lats * channels, NLON), lambda e: (e, 0, 0)),
        scratch_shapes=[
            pltpu.VMEM((groups, 2 * local * round_up(lanes_of, 8), depth), jnp.float32),
            pltpu.VMEM((pl.cdiv(NLON, 128), lanes_of * (channels + PAD), 128), jnp.float32),
        ],
        compiler_params=pltpu.CompilerParams(vmem_limit_bytes=VMEM_LIMIT),
        cost_estimate=pl.CostEstimate(
            flops=6 * local * groups * lanes_of * 2 * depth * NLON,
            transcendentals=0,
            bytes_accessed=8 * local * lats * channels * NLON,
        ),
    )(received, high, low, *parts)
    return out.reshape(local, lats, channels, NLON).transpose(0, 2, 1, 3)


def longitude_basis(orders):
    cols = jnp.arange(NLON, dtype=jnp.int32)
    phase = orders[:, None] * cols[None, :] % NLON
    angle = 2.0 * jnp.pi * phase.astype(jnp.float32) / NLON
    valid = (orders <= LMAX)[:, None]
    scale = 2.0 * jnp.pi / NLON
    cosine = jnp.where(valid, jnp.cos(angle), 0.0) * scale
    sine = jnp.where(valid, -jnp.sin(angle), 0.0) * scale
    value = jnp.concatenate([cosine, sine], axis=0)
    high = lax.reduce_precision(value, 8, 7)
    return high.astype(jnp.bfloat16), (value - high).astype(jnp.bfloat16)


def shards(members, target, order_table):
    local, channels, _, slots, degrees = members.shape
    spaces = lax.axis_size("space")
    groups = lax.axis_size("member")
    chunks = channels // groups
    me = lax.axis_index("member")
    padded = round_up(slots, 16)
    lats = (NLAT + spaces - 1) // spaces
    width = round_up(spaces * lats, 128)
    lanes_of = width // spaces

    by_device = jnp.pad(
        order_table.reshape(spaces, slots), ((0, 0), (0, padded - slots)), constant_values=LMAX + 1
    )
    mine = lax.dynamic_index_in_dim(by_device, lax.axis_index("space"), 0, keepdims=False)
    column = jnp.arange(width, dtype=jnp.int32)
    inner = column % lanes_of
    lat_index = column // lanes_of * lats + inner
    valid = (inner < lats) & (lat_index < NLAT)

    def pieces(source, chunk, bounds):
        picked = lax.rem(me + jnp.arange(groups, dtype=jnp.int32), groups) * chunks + chunk
        return cut_pieces(source, picked.astype(jnp.int32), bounds)

    def exchange(cut):
        return [cut[0]] + [
            lax.ppermute(cut[step], "member", [(i, (i + step) % groups) for i in range(groups)])
            for step in range(1, groups)
        ]

    lat_rows = jnp.where(valid, lat_index, 0)
    head = round_up(padded // 2, 8)
    items = [(0, 0, head), (0, head, padded)] + [(chunk, 0, padded) for chunk in range(1, chunks)]
    index = me.reshape(1).astype(jnp.int32)

    arrived = []
    early = pieces(members, 0, [item[1:] for item in items[:2]])
    for cut in early:
        arrived.append(exchange(cut))
    for number, (chunk, first, last) in enumerate(items[2:], 2):
        cut = pieces(members, chunk, [(first, last)])[0]
        cut, arrived[-1] = lax.optimization_barrier((cut, arrived[-1]))
        arrived.append(exchange(cut))

    tables = {}
    received = []
    for number, (chunk, first, last) in enumerate(items):
        count = min(last, slots) - first
        place = (target, chunk, first // 8)
        if number == 0:
            tables[0] = legendre_tables(mine[first:last], degrees, lat_rows, valid)
        if number == 1:
            build = table_inputs(mine[first:last], degrees, lat_rows, valid)
            payload, tables[1] = lat_payload(
                index, count, arrived[number], *place, None, spaces, build
            )
        else:
            used = [tables[0]] if number == 0 else [tables[0], tables[1]]
            payload = lat_payload(index, count, arrived[number], *place, used, spaces)
        if number == 0:
            payload, mine = lax.optimization_barrier((payload, mine))
        blocks = payload.reshape(groups * spaces, last - first, payload.shape[3])
        moved = lax.all_to_all(blocks, ("member", "space"), 0, 0, tiled=True)
        received.append(moved.reshape(groups, spaces * (last - first), payload.shape[3]))

    bases = [
        longitude_basis(by_device[:, first:last].reshape(-1)) for _, first, last in items[:2]
    ]
    full = longitude_basis(by_device.reshape(-1))
    half = local * lanes_of
    outputs = [to_longitudes(received[:2], bases, half)]
    outputs += [to_longitudes([got], [full], half) for got in received[2:-1]]
    return merge(received[-1], *full, outputs, local, lats, lanes_of)


def solution(mesh):
    placed = (P("member", None, None, "space", None), P("member", None, "space", None), P())

    return jax.shard_map(
        shards,
        mesh=mesh,
        in_specs=placed,
        out_specs=P("member", None, "space", None),
        check_vma=False,
    )
```

```python
import functools
import math

import jax
import jax.numpy as jnp
from jax import lax
from jax.experimental import pallas as pl
from jax.experimental.pallas import tpu as pltpu
from jax.sharding import PartitionSpec as P


LMAX = 360
NLAT = 361
NLON = 720

EPS = 0.01
LOG_GAMMA_HALF = 0.5 * math.log(math.pi) - math.log(2.0)
STEP_EXP = 64.0
SMALL = 2.0**-64
BIG = 2.0**32
PAD = 8
VMEM_LIMIT = 67_000_000


def round_up(value, multiple):
    return (value + multiple - 1) // multiple * multiple


def split(value):
    high = value.astype(jnp.bfloat16)
    low = (value - high.astype(jnp.float32)).astype(jnp.bfloat16)
    return high, low


def dot(a, b, dims=(((1,), (0,)), ((), ()))):
    return lax.dot_general(a, b, dims, preferred_element_type=jnp.float32)


def table_kernel(step_ref, inv_ref, order_ref, value_ref, scale_ref, cos_ref, high_ref, low_ref, rows_ref):
    group, width = value_ref.shape
    degrees = high_ref.shape[1]
    pitch = degrees + PAD
    order = order_ref[...]
    order_sq = order * order
    cosine = jnp.broadcast_to(cos_ref[0:1, :], (group, width))

    def wide(column):
        return jnp.concatenate([column] * (width // 128), axis=1)

    order_w = wide(order)

    def factors(scale):
        one = jnp.where(scale < -0.5, jnp.where(scale < -2.5, 0.0, SMALL), 1.0)
        two = jnp.where(scale < -1.5, SMALL, 1.0)
        return one, two

    def block(index, carry):
        prev, prev2, scale, root, gap = carry
        big = (jnp.maximum(jnp.abs(prev), jnp.abs(prev2)) > BIG) & (scale < -0.5)
        prev = jnp.where(big, prev * SMALL, prev)
        prev2 = jnp.where(big, prev2 * SMALL, prev2)
        scale = jnp.where(big, scale + 1.0, scale)
        one, two = factors(scale)
        for sub in range(8):
            degree = index * 8 + sub
            deg_f = degree.astype(jnp.float32)
            gap_now = deg_f * deg_f - order_sq
            root_now = lax.rsqrt(jnp.maximum(gap_now, 1.0))
            coef_a = step_ref[degree] * root_now
            coef_b = jnp.maximum(gap, 0.0) * root * inv_ref[degree]
            current = wide(coef_a) * (cosine * prev - wide(coef_b) * prev2)
            current = jnp.where(order_w == deg_f, value_ref[...], current)
            shown = (current * one) * two
            for first in range(0, group, 8):
                for lane in range(0, width, 128):
                    rows_ref[lane // 128, pl.ds(first * pitch + degree, 8, pitch), :] = shown[
                        first : first + 8, lane : lane + 128
                    ]
            prev2 = prev
            prev = current
            root, gap = root_now, gap_now
        return prev, prev2, scale, root, gap

    zeros = jnp.zeros((group, width), jnp.float32)
    lax.fori_loop(
        0,
        degrees // 8,
        block,
        (zeros, zeros, scale_ref[...], jnp.ones_like(order), jnp.zeros_like(order)),
    )

    def convert(index, _):
        keep = lax.broadcasted_iota(jnp.int32, (degrees, 128), 0) <= LMAX
        start = pl.multiple_of(index * pitch, 8)
        for tile in range(width // 128):
            value = jnp.where(keep, rows_ref[tile, pl.ds(start, degrees), :], 0.0)
            high, low = split(value)
            lanes = slice(tile * 128, tile * 128 + 128)
            high_ref[index, :, lanes] = high
            low_ref[index, :, lanes] = low
        return 0

    lax.fori_loop(0, group, convert, 0)


def table_inputs(orders, degrees, lats, valid):
    count = orders.shape[0]
    width = lats.shape[0]
    span = float(NLAT - 1)
    lat_f = lats.astype(jnp.float32)
    nearest = jnp.clip(jnp.minimum(lat_f, span - lat_f), 0.0, None)
    inside = valid & (nearest > 0.0)
    sines = jnp.where(inside, jnp.sin(jnp.pi * nearest / span), 1.0)
    cosines = jnp.cos(jnp.pi * lat_f / span)
    order_f = jnp.minimum(orders, LMAX).astype(jnp.float32)
    log_base = 0.5 * (
        math.log(1.0 / (4.0 * math.pi))
        + lax.lgamma(order_f + 1.5)
        - LOG_GAMMA_HALF
        - lax.lgamma(order_f + 1.0)
    )
    start = (log_base[:, None] + order_f[:, None] * jnp.log(sines)[None, :]) / math.log(2.0)
    scale = jnp.minimum(jnp.floor(start / STEP_EXP + 0.5), 0.0)
    weight = jnp.where(orders > LMAX, 0.0, jnp.where(orders == 0, 1.0, 2.0)).astype(jnp.float32)
    value = jnp.exp2(start - STEP_EXP * scale) * jnp.where(inside, sines, 0.0)[None, :]
    value = value * weight[:, None]
    square = jnp.arange(degrees, dtype=jnp.float32) ** 2
    step = jnp.sqrt(jnp.maximum(4.0 * square - 1.0, 1.0))
    inverse = 1.0 / jnp.concatenate([jnp.ones((1,), jnp.float32), step[:-1]])
    order_cols = jnp.broadcast_to(order_f[:, None], (count, 128))
    cos_rows = jnp.broadcast_to(cosines[None, :], (8, width))
    return step, inverse, order_cols, value, scale, cos_rows


def legendre_tables(orders, degrees, lats, valid):
    step, inverse, order_cols, value, scale, cos_rows = table_inputs(orders, degrees, lats, valid)
    count, width = value.shape
    group = 8
    rows = lambda cols: pl.BlockSpec((group, cols), lambda g, *_: (g, 0))
    out = pl.BlockSpec((group, degrees, width), lambda g, *_: (g, 0, 0))
    shape = jax.ShapeDtypeStruct((count, degrees, width), jnp.bfloat16)
    return pl.pallas_call(
        table_kernel,
        name="legendre_table",
        out_shape=(shape, shape),
        grid_spec=pltpu.PrefetchScalarGridSpec(
            num_scalar_prefetch=2,
            grid=(count // group,),
            in_specs=[rows(128), rows(width), rows(width), pl.BlockSpec((8, width), lambda g, *_: (0, 0))],
            out_specs=(out, out),
            scratch_shapes=[pltpu.VMEM((width // 128, group * (degrees + PAD), 128), jnp.float32)],
        ),
        compiler_params=pltpu.CompilerParams(vmem_limit_bytes=VMEM_LIMIT),
        cost_estimate=pl.CostEstimate(
            flops=10 * count * degrees * width,
            transcendentals=count * degrees,
            bytes_accessed=4 * count * degrees * width,
        ),
    )(step, inverse, order_cols, value, scale, cos_rows)


def cut_kernel(bounds, _, *refs):
    count = len(refs) // (1 + len(bounds))
    for index, source in enumerate(refs[:count]):
        together, slots = source.shape[:2]
        for cut, (first, last) in enumerate(bounds):
            rows = min(last, slots) - first
            piece = refs[count + cut * count + index]
            for member in range(together):
                for part in range(2):
                    piece[member, part, :rows] = source[member, first : first + rows, part, :]


def cut_pieces(members, channels, bounds):
    local, _, _, slots, degrees = members.shape
    count = channels.shape[0]
    together = 2 if local % 2 == 0 else 1
    source = members.transpose(0, 1, 3, 2, 4)

    def in_spec(piece):
        return pl.BlockSpec(
            (together, None, slots, 2, degrees), lambda e, picked: (e, picked[piece], 0, 0, 0)
        )

    shapes = [(2, last - first, degrees) for first, last in bounds for _ in range(count)]
    outs = pl.pallas_call(
        functools.partial(cut_kernel, bounds),
        name="cut_pieces",
        out_shape=[jax.ShapeDtypeStruct((local, *shape), jnp.float32) for shape in shapes],
        grid_spec=pltpu.PrefetchScalarGridSpec(
            num_scalar_prefetch=1,
            grid=(local // together,),
            in_specs=[in_spec(piece) for piece in range(count)],
            out_specs=[
                pl.BlockSpec((together, *shape), lambda e, _: (e, 0, 0, 0)) for shape in shapes
            ],
        ),
        compiler_params=pltpu.CompilerParams(vmem_limit_bytes=VMEM_LIMIT),
        cost_estimate=pl.CostEstimate(
            flops=0, transcendentals=0, bytes_accessed=16 * count * local * slots * degrees
        ),
    )(channels, *[source] * count)
    return [outs[cut * count : (cut + 1) * count] for cut in range(len(bounds))]


def gradient_kernel(slots, groups, table_steps, me_ref, *refs):
    blocks = refs[:groups]
    target_ref, band_ref = refs[groups : groups + 2]
    table_refs = refs[groups + 2 : -4]
    out_ref, sums_ref, grads_ref, lat_ref = refs[-4:]
    local = blocks[0].shape[0]
    degrees = target_ref.shape[2]
    width = band_ref.shape[1]
    spaces = out_ref.shape[1]
    width_out = out_ref.shape[3]
    count = groups * local
    rows = 2 * count
    pitch = rows + PAD
    per = 2 * local
    lanes_of = width // spaces
    first_slot = pl.program_id(0) * 8
    live = lax.broadcasted_iota(jnp.int32, (8, 128), 0) + first_slot < slots
    share = 1.0 / count
    pair_share = 1.0 / (count * (count - 1))

    def lane_tile(tile, _):
        lanes = pl.ds(pl.multiple_of(tile * 128, 128), 128)

        def coef(index):
            ref = blocks[index // local]
            return ref[index % local, 0, :, lanes], ref[index % local, 1, :, lanes]

        for group in range(groups):
            base = group * local
            mine = [coef(base + e) for e in range(local)]
            if group == 0:
                total = [[jnp.zeros((8, 128), jnp.float32) for _ in range(2)] for _ in range(local)]
            else:
                total = [[sums_ref[2 * (base + e) + r] for r in range(2)] for e in range(local)]

            def force(a, b):
                real, imag = a[0] - b[0], a[1] - b[1]
                inverse = lax.rsqrt(real * real + (imag * imag + EPS))
                return real * inverse, imag * inverse

            for e in range(local):
                for f in range(e + 1, local):
                    pull = force(mine[e], mine[f])
                    for r in range(2):
                        total[e][r] = total[e][r] + pull[r]
                        total[f][r] = total[f][r] - pull[r]
            for other in range(base + local, count):
                theirs = coef(other)
                sums = None if group == 0 else [sums_ref[2 * other + r] for r in range(2)]
                for e in range(local):
                    pull = force(mine[e], theirs)
                    for r in range(2):
                        total[e][r] = total[e][r] + pull[r]
                    if sums is None:
                        sums = [-pull[0], -pull[1]]
                    else:
                        sums = [sums[0] - pull[0], sums[1] - pull[1]]
                for r in range(2):
                    sums_ref[2 * other + r] = sums[r]
            goal = (target_ref[:, 0, lanes], target_ref[:, 1, lanes])
            owner = lax.rem(me_ref[0] + (groups - group), groups)
            for e in range(local):
                pull = force(mine[e], goal)
                for r in range(2):
                    grad = pull[r] * share - total[e][r] * pair_share
                    grad = jnp.where(live, grad, 0.0)
                    grads_ref[tile, pl.ds(owner * per + r * local + e, 8, pitch), :] = grad
        return 0

    lax.fori_loop(0, degrees // 128, lane_tile, 0)

    def transform(high_ref, low_ref):
        def one(slot, _):
            start = pl.multiple_of(slot * pitch, 8)
            grad = jnp.concatenate(
                [grads_ref[tile, pl.ds(start, rows), :] for tile in range(degrees // 128)], axis=1
            )
            high, low = split(grad)
            both = dot(jnp.concatenate([high, low], axis=0), high_ref[slot])
            lat = both[:rows] + both[rows:] + dot(high, low_ref[slot])
            for tile in range(width // 128):
                lat_ref[tile, pl.ds(start, rows), :] = lat[:, tile * 128 : tile * 128 + 128]
            return 0

        lax.fori_loop(0, 8, one, 0, unroll=8 if len(table_steps) == 1 else 4)

    if len(table_steps) == 1:
        transform(*table_refs)
    else:
        first = 0
        for index, steps in enumerate(table_steps):
            here = (pl.program_id(0) >= first) & (pl.program_id(0) < first + steps)
            pl.when(here)(functools.partial(transform, *table_refs[2 * index : 2 * index + 2]))
            first += steps

    band = band_ref[...]

    def load(group, row):
        parts = [
            lat_ref[tile, pl.ds(group * per + row, 8, pitch), :] for tile in range(width // 128)
        ]
        return jnp.concatenate(parts, axis=1)

    def scatter(group, _):
        source = [load(group, row) for row in range(per)]
        if spaces == per and width == width_out:
            distance = per // 2
            while distance:
                upper = (band & distance) != 0
                for i in range(per):
                    if i & distance:
                        continue
                    j = i | distance
                    shift = distance * lanes_of
                    from_j = pltpu.roll(source[j], shift, 1)
                    from_i = pltpu.roll(source[i], width - shift, 1)
                    source[i], source[j] = (
                        jnp.where(upper, from_j, source[i]),
                        jnp.where(upper, source[j], from_i),
                    )
                distance //= 2
            for space in range(spaces):
                out_ref[group, space] = source[space]
        else:
            for space in range(spaces):
                value = jnp.zeros((8, width_out), jnp.float32)
                for row in range(per):
                    shift = (row - space) * lanes_of % width
                    moved = source[row] if shift == 0 else pltpu.roll(source[row], shift, 1)
                    value = jnp.where(band[:, :width_out] == row, moved[:, :width_out], value)
                out_ref[group, space] = value
        return 0

    lax.fori_loop(0, groups, scatter, 0, unroll=groups if spaces == per else 1)


def fused_kernel(slots, groups, me_ref, step_ref, inv_ref, *refs):
    blocks, rest = refs[:groups], refs[groups:]
    target_ref, band_ref, order_ref, value_ref, scale_ref, cos_ref = rest[:6]
    out_ref, high_ref, low_ref, sums_ref, grads_ref, lat_ref, rows_ref = rest[6:]
    table_kernel(
        step_ref, inv_ref, order_ref, value_ref, scale_ref, cos_ref, high_ref, low_ref, rows_ref
    )
    gradient_kernel(
        slots, groups, (1,), me_ref, *blocks, target_ref, band_ref, high_ref, low_ref,
        out_ref, sums_ref, grads_ref, lat_ref,
    )


def lat_payload(me, slots, parts, targets, channel, first_step, tables, spaces, build=None):
    local, _, _, degrees = parts[0].shape
    groups = len(parts)
    if build is None:
        width = tables[0][0].shape[2]
        steps = [high.shape[0] // 8 for high, _ in tables]
    else:
        count_rows, width = build[3].shape
        steps = [count_rows // 8]
    padded = 8 * sum(steps)
    per = 2 * local
    lanes_of = width // spaces
    width_out = round_up(per * lanes_of, 128)
    count = groups * local
    band = jnp.broadcast_to((jnp.arange(width, dtype=jnp.int32) // lanes_of)[None], (8, width))
    part_spec = pl.BlockSpec((local, 2, 8, degrees), lambda g, *_: (0, 0, g, 0))
    in_specs = [part_spec] * groups + [
        pl.BlockSpec((None, 8, 2, degrees), lambda g, *_: (channel, g + first_step, 0, 0)),
        pl.BlockSpec((8, width), lambda g, *_: (0, 0)),
    ]
    out_shape = [jax.ShapeDtypeStruct((groups, spaces, padded, width_out), jnp.float32)]
    out_specs = [pl.BlockSpec((groups, spaces, 8, width_out), lambda g, *_: (0, 0, g, 0))]
    scratch = [
        pltpu.VMEM((2 * count, 8, 128), jnp.float32),
        pltpu.VMEM((degrees // 128, 8 * (2 * count + PAD), 128), jnp.float32),
        pltpu.VMEM((width // 128, 8 * (2 * count + PAD), 128), jnp.float32),
    ]
    scalars = (me,)
    if build is None:
        kernel = functools.partial(gradient_kernel, slots, groups, tuple(steps))
        before = 0
        for size in steps:
            index = lambda g, *_, size=size, before=before: (jnp.clip(g - before, 0, size - 1), 0, 0)
            in_specs += [pl.BlockSpec((8, degrees, width), index)] * 2
            before += size
        extra = [array for pair in tables for array in pair]
    else:
        kernel = functools.partial(fused_kernel, slots, groups)
        scalars += build[:2]
        extra = list(build[2:])
        rows = lambda cols: pl.BlockSpec((8, cols), lambda g, *_: (g, 0))
        in_specs += [rows(128), rows(width), rows(width), pl.BlockSpec((8, width), lambda g, *_: (0, 0))]
        out_shape += [jax.ShapeDtypeStruct((padded, degrees, width), jnp.bfloat16)] * 2
        out_specs += [pl.BlockSpec((8, degrees, width), lambda g, *_: (g, 0, 0))] * 2
        scratch.append(pltpu.VMEM((width // 128, 8 * (degrees + PAD), 128), jnp.float32))
    pairs = count * (count + 1) // 2
    outs = pl.pallas_call(
        kernel,
        name="loss_gradient",
        out_shape=out_shape,
        grid_spec=pltpu.PrefetchScalarGridSpec(
            num_scalar_prefetch=len(scalars),
            grid=(padded // 8,),
            in_specs=in_specs,
            out_specs=out_specs,
            scratch_shapes=scratch,
        ),
        compiler_params=pltpu.CompilerParams(vmem_limit_bytes=VMEM_LIMIT),
        cost_estimate=pl.CostEstimate(
            flops=6 * 2 * count * padded * degrees * width,
            transcendentals=pairs * padded * degrees,
            bytes_accessed=4 * padded * degrees * width + 16 * count * padded * degrees,
        ),
    )(*scalars, *parts, targets.transpose(0, 2, 1, 3), band, *extra)
    return outs[0] if build is None else (outs[0], (outs[1], outs[2]))


def longitude_kernel(count, *refs):
    out_ref = refs[-1]
    half = out_ref.shape[0]
    total = None
    for index in range(count):
        value = refs[index][...].T
        both = jnp.concatenate([value[:half], value[half : 2 * half]], axis=1)
        high, low = split(both)
        basis_high, basis_low = refs[count + 2 * index][...], refs[count + 2 * index + 1][...]
        part = dot(high, basis_high) + dot(low, basis_high) + dot(high, basis_low)
        total = part if total is None else total + part
    out_ref[...] = total


def to_longitudes(received, bases, half):
    groups, _, width = received[0].shape
    whole = lambda array: pl.BlockSpec(array.shape, lambda g: (0, 0))
    flat = [array for pair in bases for array in pair]
    depth = sum(array.shape[1] for array in received)
    return pl.pallas_call(
        functools.partial(longitude_kernel, len(received)),
        name="longitudes",
        out_shape=jax.ShapeDtypeStruct((groups, half, NLON), jnp.float32),
        grid=(groups,),
        in_specs=[pl.BlockSpec((None, *array.shape[1:]), lambda g: (g, 0, 0)) for array in received]
        + [whole(array) for array in flat],
        out_specs=pl.BlockSpec((None, half, NLON), lambda g: (g, 0, 0)),
        compiler_params=pltpu.CompilerParams(vmem_limit_bytes=VMEM_LIMIT),
        cost_estimate=pl.CostEstimate(
            flops=6 * groups * half * 2 * depth * NLON,
            transcendentals=0,
            bytes_accessed=4 * groups * (depth * width + half * NLON),
        ),
    )(*received, *flat)


def merge_kernel(lats, lanes_of, got_ref, high_ref, low_ref, *refs):
    ins, (out_ref, turned_ref, wide_ref) = refs[:-3], refs[-3:]
    groups, _, _ = got_ref.shape
    chunks = len(ins) + 1
    channels = groups * chunks
    local = pl.num_programs(0)
    spread = round_up(lanes_of, 8)
    pitch = channels + PAD
    member = pl.program_id(0)

    @pl.when(member == 0)
    def _():
        for group in range(groups):
            turned = got_ref[group].T
            for piece in range(turned_ref.shape[1] // spread):
                turned_ref[group, piece * spread : piece * spread + lanes_of, :] = turned[
                    piece * lanes_of : (piece + 1) * lanes_of
                ]

    def part(group, side):
        start = pl.multiple_of((side * local + member) * spread, 8)
        return turned_ref[group, pl.ds(start, lanes_of), :]

    rows = [jnp.concatenate([part(group, 0), part(group, 1)], axis=1) for group in range(groups)]
    high, low = split(jnp.concatenate(rows, axis=0))
    last = dot(high, high_ref[...]) + dot(low, high_ref[...]) + dot(high, low_ref[...])

    def place(value, channel, first, lane):
        rows, size = value.shape
        if size < 128:
            value = jnp.concatenate([value, jnp.zeros((rows, 128 - size), jnp.float32)], axis=1)
        wide_ref[lane // 128, pl.ds(first * pitch + channel, rows, pitch), :] = value

    for lane in range(0, NLON, 128):
        size = min(128, NLON - lane)
        for group in range(groups):
            for first in range(0, lanes_of, 8):
                rows = min(8, lanes_of - first)
                for chunk in range(chunks - 1):
                    value = ins[chunk][group, pl.ds(first, rows), lane : lane + size]
                    place(value, group * chunks + chunk, first, lane)
                value = last[group * lanes_of + first :, lane : lane + size][:rows]
                place(value, group * chunks + chunks - 1, first, lane)
        for lat in range(lats):
            out_ref[lat * channels : (lat + 1) * channels, lane : lane + size] = wide_ref[
                lane // 128, lat * pitch : lat * pitch + channels, :size
            ]


def merge(received, high, low, parts, local, lats, lanes_of):
    groups, depth, _ = received.shape
    channels = groups * (len(parts) + 1)
    parts = [part.reshape(groups, local, lanes_of, NLON) for part in parts]
    out = pl.pallas_call(
        functools.partial(merge_kernel, lats, lanes_of),
        name="merge_channels",
        out_shape=jax.ShapeDtypeStruct((local, lats * channels, NLON), jnp.float32),
        grid=(local,),
        in_specs=[
            pl.BlockSpec(received.shape, lambda e: (0, 0, 0)),
            pl.BlockSpec(high.shape, lambda e: (0, 0)),
            pl.BlockSpec(low.shape, lambda e: (0, 0)),
        ]
        + [pl.BlockSpec((groups, None, lanes_of, NLON), lambda e: (0, e, 0, 0))] * len(parts),
        out_specs=pl.BlockSpec((None, lats * channels, NLON), lambda e: (e, 0, 0)),
        scratch_shapes=[
            pltpu.VMEM((groups, 2 * local * round_up(lanes_of, 8), depth), jnp.float32),
            pltpu.VMEM((pl.cdiv(NLON, 128), lanes_of * (channels + PAD), 128), jnp.float32),
        ],
        compiler_params=pltpu.CompilerParams(vmem_limit_bytes=VMEM_LIMIT),
        cost_estimate=pl.CostEstimate(
            flops=6 * local * groups * lanes_of * 2 * depth * NLON,
            transcendentals=0,
            bytes_accessed=8 * local * lats * channels * NLON,
        ),
    )(received, high, low, *parts)
    return out.reshape(local, lats, channels, NLON).transpose(0, 2, 1, 3)


def longitude_basis(orders):
    cols = jnp.arange(NLON, dtype=jnp.int32)
    phase = orders[:, None] * cols[None, :] % NLON
    angle = 2.0 * jnp.pi * phase.astype(jnp.float32) / NLON
    valid = (orders <= LMAX)[:, None]
    scale = 2.0 * jnp.pi / NLON
    cosine = jnp.where(valid, jnp.cos(angle), 0.0) * scale
    sine = jnp.where(valid, -jnp.sin(angle), 0.0) * scale
    value = jnp.concatenate([cosine, sine], axis=0)
    high = lax.reduce_precision(value, 8, 7)
    return high.astype(jnp.bfloat16), (value - high).astype(jnp.bfloat16)


def shards(members, target, order_table):
    local, channels, _, slots, degrees = members.shape
    spaces = lax.axis_size("space")
    groups = lax.axis_size("member")
    chunks = channels // groups
    me = lax.axis_index("member")
    padded = round_up(slots, 16)
    lats = (NLAT + spaces - 1) // spaces
    width = round_up(spaces * lats, 128)
    lanes_of = width // spaces

    by_device = jnp.pad(
        order_table.reshape(spaces, slots), ((0, 0), (0, padded - slots)), constant_values=LMAX + 1
    )
    mine = lax.dynamic_index_in_dim(by_device, lax.axis_index("space"), 0, keepdims=False)
    column = jnp.arange(width, dtype=jnp.int32)
    inner = column % lanes_of
    lat_index = column // lanes_of * lats + inner
    valid = (inner < lats) & (lat_index < NLAT)

    def pieces(source, chunk, bounds):
        picked = lax.rem(me + jnp.arange(groups, dtype=jnp.int32), groups) * chunks + chunk
        return cut_pieces(source, picked.astype(jnp.int32), bounds)

    def exchange(cut):
        return [cut[0]] + [
            lax.ppermute(cut[step], "member", [(i, (i + step) % groups) for i in range(groups)])
            for step in range(1, groups)
        ]

    lat_rows = jnp.where(valid, lat_index, 0)
    head = round_up(padded // 2, 8)
    items = [(0, 0, head), (0, head, padded)] + [(chunk, 0, padded) for chunk in range(1, chunks)]
    index = me.reshape(1).astype(jnp.int32)

    arrived = []
    early = pieces(members, 0, [item[1:] for item in items[:2]])
    for cut in early:
        arrived.append(exchange(cut))
    for number, (chunk, first, last) in enumerate(items[2:], 2):
        cut = pieces(members, chunk, [(first, last)])[0]
        cut, arrived[-1] = lax.optimization_barrier((cut, arrived[-1]))
        arrived.append(exchange(cut))

    tables = {}
    received = []
    for number, (chunk, first, last) in enumerate(items):
        count = min(last, slots) - first
        place = (target, chunk, first // 8)
        if number == 0:
            tables[0] = legendre_tables(mine[first:last], degrees, lat_rows, valid)
        if number == 1:
            build = table_inputs(mine[first:last], degrees, lat_rows, valid)
            payload, tables[1] = lat_payload(
                index, count, arrived[number], *place, None, spaces, build
            )
        else:
            used = [tables[0]] if number == 0 else [tables[0], tables[1]]
            payload = lat_payload(index, count, arrived[number], *place, used, spaces)
        if number == 0:
            payload, mine = lax.optimization_barrier((payload, mine))
        blocks = payload.reshape(groups * spaces, last - first, payload.shape[3])
        moved = lax.all_to_all(blocks, ("member", "space"), 0, 0, tiled=True)
        received.append(moved.reshape(groups, spaces * (last - first), payload.shape[3]))

    bases = [
        longitude_basis(by_device[:, first:last].reshape(-1)) for _, first, last in items[:2]
    ]
    full = longitude_basis(by_device.reshape(-1))
    half = local * lanes_of
    outputs = [to_longitudes(received[:2], bases, half)]
    outputs += [to_longitudes([got], [full], half) for got in received[2:-1]]
    return merge(received[-1], *full, outputs, local, lats, lanes_of)


def solution(mesh):
    placed = (P("member", None, None, "space", None), P("member", None, "space", None), P())

    return jax.shard_map(
        shards,
        mesh=mesh,
        in_specs=placed,
        out_specs=P("member", None, "space", None),
        check_vma=False,
    )
```
